512 devices in a mesh: role: 2 (over y_hi), dp: 8 (over x, core), hidden: 32 (over z, y_lo).
Axes of the slice: x: 4, y: 4 (y_hi: 2, y_lo: 2; y = y_hi * 2 + y_lo), z: 16, core: 2. Of those that a mesh axis runs over, the one named last changes fastest.
Arguments:
- token_rows: bfloat16 [2, 1024, 5120], P('role', 'dp'), may hold values from -6 to 6
- cotangent: bfloat16 [1024, 5120], P('dp'), may hold values from -6 to 6
- staleness: int32 [1024], P('dp'), may hold values from 0 to 7
- prefill_rows: int32 [8], P('dp'), may hold values from 1 to 128, as said below
- frozen_gate_up_weight: bfloat16 [2, 5120, 13824], P(None, ('role', 'dp'), 'hidden'), may hold values from -0.078125 to 0.078125
- down_weight: bfloat16 [13824, 5120], P('hidden', ('role', 'dp')), may hold values from -0.0546875 to 0.0546875
- adapter_in: float32 [2, 5120, 32], P(None, 'hidden'), may hold values from -0.078125 to 0.078125
- adapter_out: float32 [2, 32, 13824], P(None, None, 'hidden'), may hold values from -0.6 to 0.6
- moment_in: float32 [2, 5120, 32], P(None, 'hidden'), may hold values from -549.5361 to 549.5361
- square_in: float32 [2, 5120, 32], P(None, 'hidden'), may hold values from 20.97152 to 2097.152
- moment_out: float32 [2, 32, 13824], P(None, None, 'hidden'), may hold values from -1.2 to 1.2
- square_out: float32 [2, 32, 13824], P(None, None, 'hidden'), may hold values from 0.01 to 1
Outputs:
- layer_old: bfloat16 [2, 1024, 5120], P('role', 'dp', 'hidden')
- layer_new: bfloat16 [2, 1024, 5120], P('role', 'dp', 'hidden')
- new_adapter_in: float32 [2, 2, 5120, 32], P('role', None, 'hidden')
- new_adapter_out: float32 [2, 2, 32, 13824], P('role', None, None, 'hidden')
- new_moment_in: float32 [2, 2, 5120, 32], P('role', None, 'hidden')
- new_square_in: float32 [2, 2, 5120, 32], P('role', None, 'hidden')
- new_moment_out: float32 [2, 2, 32, 13824], P('role', None, None, 'hidden')
- new_square_out: float32 [2, 2, 32, 13824], P('role', None, None, 'hidden')
The draws below stay inside these ranges and needn't reach their ends.
Inputs may be any that keep to these rules, and one draw needn't show every extreme that they name: The first prefill_rows[g] rows of rollout group g are live, the rest are padding; some group is full in every draw.
All inputs are finite; a program needn't handle non-finite values.
Results may differ from the reference program's by a relative error of at most 0.025.
Values may be sent and summed in bfloat16 or wider, within the bound.
No kernel may reach another device: no remote copies, remote signals or barrier semaphores. Data moves between devices by JAX's collectives and lax.ppermute only.
A program may use at most 128 MiB of HBM per device.

```python
import math
import jax
import jax.numpy as jnp
from jax import lax

D = 5120
FF = 13824
R = 32
GROUP_ROWS = 128
OPT_STEP = 10
ROWS = 1024
N_DP = 8
N_HIDDEN = 32


def draw_prefill_rows(key, part):
    base = jax.random.fold_in(key, 11)
    first_key, second_key = jax.random.split(base)
    counts = jax.random.randint(first_key, (N_DP,), 1, GROUP_ROWS + 1)
    full_group = jax.random.randint(second_key, (), 0, N_DP)
    return jnp.where(jnp.arange(N_DP) == full_group, GROUP_ROWS, counts).astype(jnp.int32)


def plant(array, own_key, least, high):
    longest = array.shape.index(max(array.shape))
    spots = []
    for shift in (0, 1):
        where = [jax.random.randint(jax.random.fold_in(own_key, axis), (), 0, length) for axis, length in enumerate(array.shape)]
        where[longest] = (where[longest] + shift) % array.shape[longest]
        spots.append(tuple(where))
    return array.at[spots[0]].set(least).at[spots[1]].set(high)


def shard_levels(own_key, extent, cuts, smallest, top_value):
    level = 1.0
    for axis_at, shards_of in cuts:
        draws = jax.random.uniform(jax.random.fold_in(jax.random.fold_in(own_key, 6), axis_at), (shards_of,), jnp.float32, smallest / len(cuts), top_value / len(cuts))
        level = level * jnp.repeat(jnp.exp(draws), extent[axis_at] // shards_of).reshape((-1,) + (1,) * (len(extent) - 1 - axis_at))
    return level


def centred(rng, shape, deviation, most, cuts=(), kind=jnp.bfloat16):
    values = deviation * jax.random.normal(rng, shape, jnp.float32)
    if cuts:
        values = values * shard_levels(rng, shape, cuts, -0.22, 0.18)
    return jnp.clip(values, -most, most).astype(kind)


def setup_inputs(seed: int = 0) -> dict:
    key_of = jax.random.split(jax.random.key(seed), 13)
    token_rows = centred(key_of[0], (2, ROWS, D), 1.0, 6.0, ((0, 2), (1, 8)))
    cotangent = centred(key_of[1], (ROWS, D), 1.0, 6.0, ((0, 8),))
    staleness = plant(jax.random.randint(key_of[2], (ROWS,), 0, 8), jax.random.fold_in(key_of[2], 1), 0, 7).astype(jnp.int32)
    prefill_rows = draw_prefill_rows(jax.random.fold_in(key_of[12], 71), 0)
    frozen_gate_up_weight = centred(key_of[4], (2, D, FF), D ** -0.5, 0.078125, ((1, 16), (2, 32)))
    down_weight = centred(key_of[5], (FF, D), FF ** -0.5, 0.0546875, ((0, 32), (1, 16)))
    adapter_in = centred(key_of[6], (2, D, R), D ** -0.5, 0.078125, ((1, 32),), jnp.float32)
    adapter_out = centred(key_of[7], (2, R, FF), 0.1, 0.6, ((2, 32),), jnp.float32)
    moment_in = centred(key_of[8], (2, D, R), (0.04 * (ROWS * D) ** 0.5), 549.5361, ((1, 32),), jnp.float32)
    square_in = jnp.clip(jnp.exp(math.log(2097.152) - 4.6051703 * jax.random.uniform(key_of[9], (2, D, R), jnp.float32) ** shard_levels(key_of[9], (2, D, R), ((1, 32),), -0.2, 0.2)), 20.97152, 2097.152)
    moment_out = centred(key_of[10], (2, R, FF), 0.2, 1.2, ((2, 32),), jnp.float32)
    square_out = jnp.clip(jnp.exp(math.log(1.0) - 4.6051702 * jax.random.uniform(key_of[11], (2, R, FF), jnp.float32) ** shard_levels(key_of[11], (2, R, FF), ((2, 32),), -0.2, 0.2)), 0.01, 1.0)
    return dict(token_rows=token_rows, cotangent=cotangent, staleness=staleness, prefill_rows=prefill_rows, frozen_gate_up_weight=frozen_gate_up_weight, down_weight=down_weight, adapter_in=adapter_in, adapter_out=adapter_out, moment_in=moment_in, square_in=square_in, moment_out=moment_out, square_out=square_out)


ADAPTER_SCALE = 2.0
BETA_ONE = 0.9
BETA_TWO = 0.999
RATE_FACTOR = 0.34
ADAM_EPS = 1e-08
KEEP_RATE = 0.75

def adam_update(param, grad, first, second):
    learn_rate = RATE_FACTOR / D ** 0.5
    first_new = BETA_ONE * first + (1.0 - BETA_ONE) * grad
    second_new = BETA_TWO * second + (1.0 - BETA_TWO) * grad * grad
    first_fix = first_new / (1.0 - BETA_ONE ** OPT_STEP)
    second_fix = second_new / (1.0 - BETA_TWO ** OPT_STEP)
    return (param - learn_rate * first_fix / (jnp.sqrt(second_fix) + ADAM_EPS), first_new, second_new)

def down_sum(hidden_act, down_weight):
    width = FF // N_HIDDEN
    total = jnp.zeros((hidden_act.shape[0], D), jnp.float32)
    for segment in range(N_HIDDEN):
        partial_value = jnp.dot(hidden_act[:, segment * width:(segment + 1) * width], down_weight[segment * width:(segment + 1) * width], preferred_element_type=jnp.float32)
        rounded = lax.optimization_barrier(partial_value.astype(jnp.bfloat16))
        total = total + rounded.astype(jnp.float32)
    return total.astype(jnp.bfloat16)

def twice(value):
    return jnp.stack([value, value])

def reference(token_rows, cotangent, staleness, prefill_rows, frozen_gate_up_weight, down_weight, adapter_in, adapter_out, moment_in, square_in, moment_out, square_out):
    in_bf = adapter_in.astype(jnp.bfloat16)
    out_bf = adapter_out.astype(jnp.bfloat16)
    positions = jnp.arange(ROWS)
    limit = jnp.take(prefill_rows, positions // GROUP_ROWS)
    live = positions % GROUP_ROWS < limit
    old_list = []
    for half in range(2):
        token_batch = token_rows[half]
        reduced_gradient = jnp.einsum('rd,kdq->krq', token_batch.astype(jnp.float32), in_bf.astype(jnp.float32)).astype(jnp.bfloat16)
        lifted_rows = jnp.einsum('krq,kqf->krf', reduced_gradient.astype(jnp.float32), out_bf.astype(jnp.float32))
        gate_preactivation = jnp.dot(token_batch, frozen_gate_up_weight[0], preferred_element_type=jnp.float32) + ADAPTER_SCALE * lifted_rows[0]
        up_preactivation = jnp.dot(token_batch, frozen_gate_up_weight[1], preferred_element_type=jnp.float32) + ADAPTER_SCALE * lifted_rows[1]
        hidden_act = (jax.nn.silu(gate_preactivation) * up_preactivation).astype(jnp.bfloat16)
        result = down_sum(hidden_act, down_weight)
        if half == 1:
            result = jnp.where(live[:, None], result, jnp.zeros_like(result))
        else:
            saved = (token_batch, reduced_gradient, gate_preactivation, up_preactivation)
        old_list.append(result)
    token_batch, reduced_gradient, gate_preactivation, up_preactivation = saved
    row_weight = KEEP_RATE ** staleness.astype(jnp.float32)
    upstream = (row_weight[:, None] * cotangent.astype(jnp.float32)).astype(jnp.bfloat16)
    grad_hidden = lax.dot_general(upstream, down_weight, (((1,), (1,)), ((), ())), preferred_element_type=jnp.float32)
    sigma = jax.nn.sigmoid(gate_preactivation)
    grad_gate = (grad_hidden * up_preactivation * sigma * (1.0 + gate_preactivation * (1.0 - sigma))).astype(jnp.bfloat16)
    grad_up = (grad_hidden * gate_preactivation * sigma).astype(jnp.bfloat16)
    gradient_tree = jnp.stack([grad_gate, grad_up]).astype(jnp.float32)
    adapter_out_gradient = ADAPTER_SCALE * jnp.einsum('aod,aot->adt', reduced_gradient.astype(jnp.float32), gradient_tree)
    passed_through = jnp.einsum('krf,kqf->krq', gradient_tree, out_bf.astype(jnp.float32)).astype(jnp.bfloat16)
    adapter_in_gradient = ADAPTER_SCALE * jnp.einsum('un,huj->hnj', token_batch.astype(jnp.float32), passed_through.astype(jnp.float32))
    new_in, new_m_in, new_s_in = adam_update(adapter_in, adapter_in_gradient, moment_in, square_in)
    new_out, new_m_out, new_s_out = adam_update(adapter_out, adapter_out_gradient, moment_out, square_out)
    updated_in_brainfloat = new_in.astype(jnp.bfloat16)
    updated_out_brainfloat = new_out.astype(jnp.bfloat16)
    merged_weight = []
    for group_member in range(2):
        merged_weight.append((frozen_gate_up_weight[group_member].astype(jnp.float32) + ADAPTER_SCALE * jnp.dot(updated_in_brainfloat[group_member], updated_out_brainfloat[group_member], preferred_element_type=jnp.float32)).astype(jnp.bfloat16))
    new_list = []
    for half in range(2):
        token_batch = token_rows[half]
        gate_post = jnp.dot(token_batch, merged_weight[0], preferred_element_type=jnp.float32)
        up_post = jnp.dot(token_batch, merged_weight[1], preferred_element_type=jnp.float32)
        hidden_act = (jax.nn.silu(gate_post) * up_post).astype(jnp.bfloat16)
        result = down_sum(hidden_act, down_weight)
        if half == 1:
            result = jnp.where(live[:, None], result, jnp.zeros_like(result))
        new_list.append(result)
    return (jnp.stack(old_list), jnp.stack(new_list), twice(new_in), twice(new_out), twice(new_m_in), twice(new_s_in), twice(new_m_out), twice(new_s_out))
```

```python
import jax
import jax.numpy as jnp
from jax import lax
from jax.experimental import pallas as pl
from jax.experimental.pallas import tpu as pltpu
from jax.sharding import Mesh
from jax.sharding import PartitionSpec as P

D = 5120
OPT_STEP = 10

ADAPTER_SCALE = 2.0
BETA_ONE = 0.9
BETA_TWO = 0.999
RATE_FACTOR = 0.34
ADAM_EPS = 1e-08
KEEP_RATE = 0.75

DP = ("x", "core")
ALL_GROUPS = ("role", "x", "core")
NEAR = ("zl", "ylo")
HIDDEN = ("zh", "zl", "ylo")
ALONG = ("zh", "zl")
BF = jnp.bfloat16
F32 = jnp.float32


VMEM = pl.BlockSpec(memory_space=pltpu.VMEM)
SMEM = pl.BlockSpec(memory_space=pltpu.SMEM)
ANY = pl.BlockSpec(memory_space=pl.ANY)


def exchange(pieces, axis):
    return lax.all_to_all(pieces, axis, split_axis=0, concat_axis=0, tiled=True)


def swapped(value, axis):
    return lax.ppermute(value, axis, [(0, 1), (1, 0)])


def spread(value, axis):
    count = lax.axis_size(axis)
    return exchange(jnp.broadcast_to(value, (count, *value.shape)), axis)


def sum_first(pieces):
    return pieces.astype(F32).sum(axis=0)


def hidden_total(value):
    near = sum_first(spread(value.astype(BF), NEAR)).astype(BF)
    return sum_first(spread(near, "zh"))


def shifted(value, axis, step):
    count = lax.axis_size(axis)
    return lax.ppermute(value, axis, [(i, (i + step) % count) for i in range(count)])


def total_by_shifts(value, axis):
    return value + sum(shifted(value, axis, step) for step in range(1, lax.axis_size(axis)))


def shifted_sum(pieces, axis):
    index = lax.axis_index(axis)
    count = lax.axis_size(axis)
    total = lax.dynamic_index_in_dim(pieces, index, 0, keepdims=False).astype(F32)
    for step in range(1, count):
        piece = lax.dynamic_index_in_dim(pieces, lax.rem(index + step, count), 0, keepdims=False)
        total = total + shifted(piece, axis, step).astype(F32)
    return total


def adam_update(param, grad, first, second):
    learn_rate = RATE_FACTOR / D**0.5
    first_new = BETA_ONE * first + (1.0 - BETA_ONE) * grad
    second_new = BETA_TWO * second + (1.0 - BETA_TWO) * grad * grad
    first_fix = first_new / (1.0 - BETA_ONE**OPT_STEP)
    second_fix = second_new / (1.0 - BETA_TWO**OPT_STEP)
    return (
        param - learn_rate * first_fix / (jnp.sqrt(second_fix) + ADAM_EPS),
        first_new,
        second_new,
    )


def dot(a, b, dims):
    return lax.dot_general(a, b, (dims, ((), ())), preferred_element_type=F32)


def rows_kernel(token_ref, cotangent_ref, scale_ref, out_ref):
    width = out_ref.shape[4]
    scale = scale_ref[...]
    for half in range(2):
        for x in range(4):
            columns = slice((half * 4 + x) * width, (half * 4 + x + 1) * width)
            out_ref[x, 0, half] = token_ref[:, columns]
            out_ref[x, 1, half] = (scale * cotangent_ref[:, columns].astype(F32)).astype(BF)


def rows_by_x(tokens, cotangent, scale):
    group, width = tokens.shape
    return pl.pallas_call(
        rows_kernel,
        out_shape=jax.ShapeDtypeStruct((4, 2, 2, group, width // 8), BF),
        in_specs=[VMEM, VMEM, VMEM],
        out_specs=VMEM,
        name="rows_by_x",
    )(tokens, cotangent, scale)


def partial_kernel(flag_ref, rows_ref, *refs):
    weight_refs, down_refs = refs[:4], refs[4:6]
    out_ref, weight, down, held, in_sems, out_sems = refs[6:]
    role, core = flag_ref[0], flag_ref[1]
    depth = weight_refs[0].shape[1]
    weight_loads, down_loads = [], []
    for i in range(2):
        side = core if i == 0 else 1 - core
        place = pl.ds(pl.multiple_of(side * depth, depth), depth)
        for j in range(2):
            half = role if j == 0 else 1 - role
            n = 2 * i + j
            down_loads.append(pltpu.make_async_copy(down_refs[i].at[j], down.at[half, place, :], in_sems.at[n]))
            weight_loads.append(pltpu.make_async_copy(weight_refs[n], weight.at[half, :, place, :], in_sems.at[4 + n]))
    for copy in down_loads + weight_loads:
        copy.start()

    count, group = rows_ref.shape[0], rows_ref.shape[3]

    def all_rows(which, half):
        return jnp.concatenate([rows_ref[x, which, half] for x in range(count)], axis=0)

    stores = []
    for k in (2, 0, 1):
        for copy in {2: down_loads, 0: weight_loads, 1: []}[k]:
            copy.wait()
        total = 0.0
        for half in range(2):
            if k < 2:
                total += dot(all_rows(0, half), weight[half, k], ((1,), (0,)))
            else:
                total += dot(all_rows(1, half), down[half], ((1,), (0,)))
        turned = total.astype(BF).T
        for x in range(count):
            held[k, x] = turned[:, x * group : (x + 1) * group]
        copy = pltpu.make_async_copy(held.at[k], out_ref.at[:, k], out_sems.at[k])
        copy.start()
        stores.append(copy)
    for copy in stores:
        copy.wait()


def partials(flags, rows, weights, downs):
    count, _, _, group, _ = rows.shape
    _, depth, cols = weights[0].shape
    return pl.pallas_call(
        partial_kernel,
        out_shape=jax.ShapeDtypeStruct((count, 3, cols, group), BF),
        in_specs=[SMEM, VMEM] + [ANY] * 6,
        out_specs=ANY,
        scratch_shapes=[
            pltpu.VMEM((2, 2, 2 * depth, cols), BF),
            pltpu.VMEM((2, 2 * depth, cols), BF),
            pltpu.VMEM((3, count, cols, group), BF),
            pltpu.SemaphoreType.DMA((8,)),
            pltpu.SemaphoreType.DMA((3,)),
        ],
        name="partials",
    )(flags, rows, *weights, *downs)


def middle_kernel(flag_ref, pieces_ref, reduced_ref, lift_ref, base_ref, hidden_ref, through_ref, grad_ref):
    total = [pieces_ref[0, k].astype(F32) for k in range(3)]
    for x in range(1, pieces_ref.shape[0]):
        for k in range(3):
            total[k] = total[k] + pieces_ref[x, k].astype(F32)
    rank = lift_ref.shape[1]
    pre = []
    for k in range(2):
        base_ref[k] = total[k]
        part = reduced_ref[k * rank : (k + 1) * rank, :]
        pre.append(total[k] + ADAPTER_SCALE * dot(lift_ref[k], part, ((0,), (0,))))
    gate, up = pre
    sigma = jax.nn.sigmoid(gate)
    silu = gate * sigma
    hidden_ref[...] = (silu * up).astype(BF)
    grad_hidden = jnp.where(flag_ref[0] == 0, total[2], jnp.zeros_like(total[2]))
    grads = (
        (grad_hidden * up * sigma * (1.0 + gate * (1.0 - sigma))).astype(BF),
        (grad_hidden * silu).astype(BF),
    )
    for k in range(2):
        block = slice(k * rank, (k + 1) * rank)
        through_ref[block, :] = dot(lift_ref[k], grads[k], ((1,), (0,))).astype(BF)
        grad_ref[block, :] = (
            ADAPTER_SCALE * dot(reduced_ref[block, :], grads[k], ((1,), (1,)))
        ).astype(BF)


def middle(flags, pieces, reduced, lift):
    _, _, cols, group = pieces.shape
    ranks = reduced.shape[0]
    return pl.pallas_call(
        middle_kernel,
        out_shape=(
            jax.ShapeDtypeStruct((2, cols, group), F32),
            jax.ShapeDtypeStruct((cols, group), BF),
            jax.ShapeDtypeStruct((ranks, group), BF),
            jax.ShapeDtypeStruct((ranks, cols), BF),
        ),
        in_specs=[SMEM, VMEM, VMEM, VMEM],
        out_specs=(VMEM, VMEM, VMEM, VMEM),
        name="middle",
    )(flags, pieces, reduced, lift)


def down_product(flag_ref, hidden, block_refs, out_ref):
    role, x, core = flag_ref[0], flag_ref[2], flag_ref[1]
    size = out_ref.shape[1]
    for i in range(2):
        side = core if i == 0 else 1 - core
        for step in range(4):
            source = lax.rem(x + 4 - step, 4)
            for j in range(2):
                half = role if j == 0 else 1 - role
                product = dot(block_refs[4 * i + step][j], hidden, ((1,), (0,))).astype(BF)
                block = half * 8 + 2 * source + side
                for s in range(2):
                    place = 2 * block + s
                    out_ref[lax.rem(place, 8) * 4 + lax.div(place, 8)] = product[s * size : (s + 1) * size]


def old_kernel(flag_ref, hidden_ref, *refs):
    down_product(flag_ref, hidden_ref[...], refs[:-1], refs[-1])


def new_kernel(flag_ref, base_ref, reduced_ref, lift_ref, *refs):
    rank = lift_ref.shape[1]
    post = []
    for k in range(2):
        part = reduced_ref[k * rank : (k + 1) * rank, :]
        post.append(base_ref[k] + ADAPTER_SCALE * dot(lift_ref[k], part, ((0,), (0,))))
    hidden = (post[0] * jax.nn.sigmoid(post[0]) * post[1]).astype(BF)
    down_product(flag_ref, hidden, refs[:-1], refs[-1])


def layer_call(kernel, name, group, width, blocks, *operands):
    return pl.pallas_call(
        kernel,
        out_shape=jax.ShapeDtypeStruct((32, width, group), BF),
        in_specs=[SMEM] + [VMEM] * (len(operands) - 1 + len(blocks)),
        out_specs=VMEM,
        name=name,
    )(*operands, *blocks)


def local(
    token_rows,
    cotangent,
    staleness,
    prefill_rows,
    frozen_gate_up_weight,
    down_weight,
    adapter_in,
    adapter_out,
    moment_in,
    square_in,
    moment_out,
    square_out,
):
    role = lax.axis_index("role")
    core = lax.axis_index("core")
    shard_index = lax.axis_index(HIDDEN)
    flags = jnp.stack([role, core, lax.axis_index("x")]).astype(jnp.int32)
    token_batch = token_rows[0]
    group_rows = token_batch.shape[0]
    slice_width = adapter_in.shape[1]
    cols = frozen_gate_up_weight.shape[2]
    token_part = lax.dynamic_slice_in_dim(token_batch, shard_index * slice_width, slice_width, 1)

    row_weight = KEEP_RATE ** staleness.astype(F32)
    rows = exchange(rows_by_x(token_batch, cotangent, row_weight[:, None]), "x")

    in_bf = adapter_in.astype(BF)
    out_bf = adapter_out.astype(BF)
    ranks = 2 * in_bf.shape[2]

    def to_rank(matrix):
        part = jnp.einsum("knq,rn->kqr", matrix, token_part, preferred_element_type=F32)
        return part.reshape(ranks, group_rows)

    reduced = to_rank(in_bf)
    reduced = total_by_shifts(reduced + swapped(reduced, "ylo"), "zl")

    other_half = swapped(frozen_gate_up_weight, "role")
    own_down = down_weight.T
    other_down = swapped(own_down, "role")
    other_half, other_down, reduced = lax.optimization_barrier((other_half, other_down, reduced))
    weights = (
        frozen_gate_up_weight,
        other_half,
        swapped(frozen_gate_up_weight, "core"),
        swapped(other_half, "core"),
    )
    down_pair = jnp.stack([own_down, other_down])
    downs = (down_pair, swapped(down_pair, "core"))
    pieces = exchange(partials(flags, rows, weights, downs), "x")
    reduced = total_by_shifts(reduced, "zh").astype(BF)
    base, hidden_old, through_part, out_part = middle(flags, pieces, reduced, out_bf)

    down_first, _ = lax.optimization_barrier((down_pair, pieces))
    through = spread(through_part, NEAR)
    through, down_later = lax.optimization_barrier((through, down_first))
    same_core = [shifted(down_first if step == 1 else down_later, "x", step) for step in range(1, 4)]

    through = sum_first(spread(sum_first(through).astype(BF), "zh")).astype(BF)
    in_part = ADAPTER_SCALE * jnp.dot(through, token_part, preferred_element_type=F32)
    packed = jnp.concatenate([out_part, in_part.astype(BF)], axis=1)
    packed, same_core = lax.optimization_barrier((packed, same_core))
    grads = spread(packed, ALL_GROUPS)
    blocks = [down_pair, *same_core, downs[1], *(swapped(b, "core") for b in same_core)]
    old_parts = layer_call(old_kernel, "old_layer", group_rows, slice_width, blocks, flags, hidden_old)
    grads, old_parts = lax.optimization_barrier((grads, old_parts))
    grads = sum_first(grads)
    grad_in = grads[:, cols:].reshape(2, -1, slice_width).transpose(0, 2, 1)
    grad_out = grads[:, :cols].reshape(2, -1, cols)
    new_in, new_m_in, new_s_in = adam_update(adapter_in, grad_in, moment_in, square_in)
    new_out, new_m_out, new_s_out = adam_update(adapter_out, grad_out, moment_out, square_out)

    positions = jnp.arange(group_rows)
    live = jnp.logical_or(role == 0, positions < prefill_rows[0])

    def finish(total):
        total = total.astype(BF).T
        return jnp.where(live[:, None], total, jnp.zeros_like(total))

    old_parts = old_parts.reshape(4, 2, 4, slice_width, group_rows)
    side = lax.axis_index("ylo")
    give = swapped(lax.dynamic_index_in_dim(old_parts, 1 - side, 1, keepdims=False), "ylo")
    keep = lax.dynamic_index_in_dim(old_parts, side, 1, keepdims=False)
    pair = (keep.astype(F32) + give.astype(F32)).astype(BF)
    renewed = hidden_total(to_rank(new_in.astype(BF))).astype(BF)
    renewed, pair = lax.optimization_barrier((renewed, pair))
    near_old = shifted_sum(pair, "zl")
    new_parts = layer_call(
        new_kernel, "new_layer", group_rows, slice_width, blocks, flags, base, renewed, new_out.astype(BF)
    )
    near_new = sum_first(exchange(new_parts.reshape(8, 4, slice_width, group_rows), NEAR))
    near = jnp.stack([near_old, near_new], axis=1).astype(BF)
    layers = sum_first(exchange(near, "zh"))
    layer_old, layer_new = finish(layers[0]), finish(layers[1])
    return (
        layer_old[None],
        layer_new[None],
        new_in[None],
        new_out[None],
        new_m_in[None],
        new_s_in[None],
        new_m_out[None],
        new_s_out[None],
    )


def solution(mesh):
    fine = Mesh(mesh.devices.reshape(2, 4, 2, 4, 4, 2), ("role", "x", "core", "zh", "zl", "ylo"))
    wide = ("role", "x", "core")
    in_specs = (
        P("role", DP, None),
        P(DP, None),
        P(DP),
        P(DP),
        P(None, wide, HIDDEN),
        P(HIDDEN, wide),
        P(None, HIDDEN, None),
        P(None, None, HIDDEN),
        P(None, HIDDEN, None),
        P(None, HIDDEN, None),
        P(None, None, HIDDEN),
        P(None, None, HIDDEN),
    )
    out_specs = (
        P("role", DP, HIDDEN),
        P("role", DP, HIDDEN),
        P("role", None, HIDDEN, None),
        P("role", None, None, HIDDEN),
        P("role", None, HIDDEN, None),
        P("role", None, HIDDEN, None),
        P("role", None, None, HIDDEN),
        P("role", None, None, HIDDEN),
    )
    return jax.shard_map(local, mesh=fine, in_specs=in_specs, out_specs=out_specs, check_vma=False)
```

```python
import jax
import jax.numpy as jnp
from jax import lax
from jax.experimental import pallas as pl
from jax.experimental.pallas import tpu as pltpu
from jax.sharding import Mesh
from jax.sharding import PartitionSpec as P


D = 5120
OPT_STEP = 10

ADAPTER_SCALE = 2.0
BETA_ONE = 0.9
BETA_TWO = 0.999
RATE_FACTOR = 0.34
ADAM_EPS = 1e-08
KEEP_RATE = 0.75

DP = ("x", "core")
ALL_GROUPS = ("role", "x", "core")
NEAR = ("zl", "ylo")
HIDDEN = ("zh", "zl", "ylo")
BF = jnp.bfloat16
F32 = jnp.float32


VMEM = pl.BlockSpec(memory_space=pltpu.VMEM)
SMEM = pl.BlockSpec(memory_space=pltpu.SMEM)
ANY = pl.BlockSpec(memory_space=pl.ANY)


def exchange(pieces, axis):
    return lax.all_to_all(pieces, axis, split_axis=0, concat_axis=0, tiled=True)


def swapped(value, axis):
    return lax.ppermute(value, axis, [(0, 1), (1, 0)])


def spread(value, axis):
    count = lax.axis_size(axis)
    return exchange(jnp.broadcast_to(value, (count, *value.shape)), axis)


def sum_first(pieces):
    return pieces.astype(F32).sum(axis=0)


def hidden_total(value):
    near = sum_first(spread(value.astype(BF), NEAR)).astype(BF)
    return sum_first(spread(near, "zh"))


def shifted(value, axis, step):
    count = lax.axis_size(axis)
    return lax.ppermute(value, axis, [(i, (i + step) % count) for i in range(count)])


def plus_partner(value, axis, step):
    count = lax.axis_size(axis)
    return value + lax.ppermute(value, axis, [(i, i ^ step) for i in range(count)])


def shifted_sum(pieces, axis):
    index = lax.axis_index(axis)
    count = lax.axis_size(axis)
    total = lax.dynamic_index_in_dim(pieces, index, 0, keepdims=False).astype(F32)
    for step in range(1, count):
        piece = lax.dynamic_index_in_dim(pieces, lax.rem(index + step, count), 0, keepdims=False)
        total = total + shifted(piece, axis, step).astype(F32)
    return total


def adam_update(param, grad, first, second):
    learn_rate = RATE_FACTOR / D**0.5
    first_new = BETA_ONE * first + (1.0 - BETA_ONE) * grad
    second_new = BETA_TWO * second + (1.0 - BETA_TWO) * grad * grad
    first_fix = first_new / (1.0 - BETA_ONE**OPT_STEP)
    second_fix = second_new / (1.0 - BETA_TWO**OPT_STEP)
    return (
        param - learn_rate * first_fix / (jnp.sqrt(second_fix) + ADAM_EPS),
        first_new,
        second_new,
    )


def dot(a, b, dims):
    return lax.dot_general(a, b, (dims, ((), ())), preferred_element_type=F32)


def rows_kernel(token_ref, cotangent_ref, scale_ref, out_ref):
    width = out_ref.shape[4]
    scale = scale_ref[...]
    for half in range(2):
        for x in range(4):
            columns = slice((half * 4 + x) * width, (half * 4 + x + 1) * width)
            out_ref[x, 0, half] = token_ref[:, columns]
            out_ref[x, 1, half] = (scale * cotangent_ref[:, columns].astype(F32)).astype(BF)


def rows_by_x(tokens, cotangent, scale):
    group, width = tokens.shape
    return pl.pallas_call(
        rows_kernel,
        out_shape=jax.ShapeDtypeStruct((4, 2, 2, group, width // 8), BF),
        in_specs=[VMEM, VMEM, VMEM],
        out_specs=VMEM,
        name="rows_by_x",
    )(tokens, cotangent, scale)


def partial_kernel(flag_ref, rows_ref, *refs):
    weight_refs, down_refs = refs[:4], refs[4:6]
    out_ref, weight, down, held, in_sems, out_sems = refs[6:]
    role, core = flag_ref[0], flag_ref[1]
    depth = weight_refs[0].shape[1]
    weight_loads, down_loads = [], []
    for i in range(2):
        side = core if i == 0 else 1 - core
        place = pl.ds(pl.multiple_of(side * depth, depth), depth)
        for j in range(2):
            half = role if j == 0 else 1 - role
            n = 2 * i + j
            down_loads.append(pltpu.make_async_copy(down_refs[i].at[j], down.at[half, place, :], in_sems.at[n]))
            weight_loads.append(pltpu.make_async_copy(weight_refs[n], weight.at[half, :, place, :], in_sems.at[4 + n]))
    for copy in down_loads + weight_loads:
        copy.start()

    count, group = rows_ref.shape[0], rows_ref.shape[3]

    def all_rows(which, half):
        return jnp.concatenate([rows_ref[x, which, half] for x in range(count)], axis=0)

    stores = []
    for k in (2, 0, 1):
        for copy in {2: down_loads, 0: weight_loads, 1: []}[k]:
            copy.wait()
        total = 0.0
        for half in range(2):
            if k < 2:
                total += dot(all_rows(0, half), weight[half, k], ((1,), (0,)))
            else:
                total += dot(all_rows(1, half), down[half], ((1,), (0,)))
        turned = total.astype(BF).T
        for x in range(count):
            held[k, x] = turned[:, x * group : (x + 1) * group]
        copy = pltpu.make_async_copy(held.at[k], out_ref.at[:, k], out_sems.at[k])
        copy.start()
        stores.append(copy)
    for copy in stores:
        copy.wait()


def partials(flags, rows, weights, downs):
    count, _, _, group, _ = rows.shape
    _, depth, cols = weights[0].shape
    return pl.pallas_call(
        partial_kernel,
        out_shape=jax.ShapeDtypeStruct((count, 3, cols, group), BF),
        in_specs=[SMEM, VMEM] + [ANY] * 6,
        out_specs=ANY,
        scratch_shapes=[
            pltpu.VMEM((2, 2, 2 * depth, cols), BF),
            pltpu.VMEM((2, 2 * depth, cols), BF),
            pltpu.VMEM((3, count, cols, group), BF),
            pltpu.SemaphoreType.DMA((8,)),
            pltpu.SemaphoreType.DMA((3,)),
        ],
        name="partials",
    )(flags, rows, *weights, *downs)


def middle_kernel(flag_ref, pieces_ref, reduced_ref, lift_ref, base_ref, hidden_ref, through_ref, grad_ref):
    total = [pieces_ref[0, k].astype(F32) for k in range(3)]
    for x in range(1, pieces_ref.shape[0]):
        for k in range(3):
            total[k] = total[k] + pieces_ref[x, k].astype(F32)
    rank = lift_ref.shape[1]
    pre = []
    for k in range(2):
        base_ref[k] = total[k]
        part = reduced_ref[k * rank : (k + 1) * rank, :]
        pre.append(total[k] + ADAPTER_SCALE * dot(lift_ref[k], part, ((0,), (0,))))
    gate, up = pre
    sigma = jax.nn.sigmoid(gate)
    silu = gate * sigma
    hidden_ref[...] = (silu * up).astype(BF)
    grad_hidden = jnp.where(flag_ref[0] == 0, total[2], jnp.zeros_like(total[2]))
    grads = (
        (grad_hidden * up * sigma * (1.0 + gate * (1.0 - sigma))).astype(BF),
        (grad_hidden * silu).astype(BF),
    )
    for k in range(2):
        block = slice(k * rank, (k + 1) * rank)
        through_ref[block, :] = dot(lift_ref[k], grads[k], ((1,), (0,))).astype(BF)
        grad_ref[block, :] = (
            ADAPTER_SCALE * dot(reduced_ref[block, :], grads[k], ((1,), (1,)))
        ).astype(BF)


def middle(flags, pieces, reduced, lift):
    _, _, cols, group = pieces.shape
    ranks = reduced.shape[0]
    return pl.pallas_call(
        middle_kernel,
        out_shape=(
            jax.ShapeDtypeStruct((2, cols, group), F32),
            jax.ShapeDtypeStruct((cols, group), BF),
            jax.ShapeDtypeStruct((ranks, group), BF),
            jax.ShapeDtypeStruct((ranks, cols), BF),
        ),
        in_specs=[SMEM, VMEM, VMEM, VMEM],
        out_specs=(VMEM, VMEM, VMEM, VMEM),
        name="middle",
    )(flags, pieces, reduced, lift)


def down_product(flag_ref, hidden, block_refs, out_ref):
    role, x, core = flag_ref[0], flag_ref[2], flag_ref[1]
    size = out_ref.shape[1]
    for i in range(2):
        side = core if i == 0 else 1 - core
        for step in range(4):
            source = lax.rem(x + 4 - step, 4)
            for j in range(2):
                half = role if j == 0 else 1 - role
                product = dot(block_refs[4 * i + step][j], hidden, ((1,), (0,))).astype(BF)
                block = half * 8 + 2 * source + side
                for s in range(2):
                    place = 2 * block + s
                    out_ref[lax.rem(place, 8) * 4 + lax.div(place, 8)] = product[s * size : (s + 1) * size]


def old_kernel(flag_ref, hidden_ref, *refs):
    down_product(flag_ref, hidden_ref[...], refs[:-1], refs[-1])


def new_kernel(flag_ref, base_ref, reduced_ref, lift_ref, *refs):
    rank = lift_ref.shape[1]
    post = []
    for k in range(2):
        part = reduced_ref[k * rank : (k + 1) * rank, :]
        post.append(base_ref[k] + ADAPTER_SCALE * dot(lift_ref[k], part, ((0,), (0,))))
    hidden = (post[0] * jax.nn.sigmoid(post[0]) * post[1]).astype(BF)
    down_product(flag_ref, hidden, refs[:-1], refs[-1])


def layer_call(kernel, group, width, blocks, *operands):
    return pl.pallas_call(
        kernel,
        out_shape=jax.ShapeDtypeStruct((32, width, group), BF),
        in_specs=[SMEM] + [VMEM] * (len(operands) - 1 + len(blocks)),
        out_specs=VMEM,
    )(*operands, *blocks)


def step(
    token_rows,
    cotangent,
    staleness,
    prefill_rows,
    frozen_gate_up_weight,
    down_weight,
    adapter_in,
    adapter_out,
    moment_in,
    square_in,
    moment_out,
    square_out,
):
    role = lax.axis_index("role")
    core = lax.axis_index("core")
    shard_index = lax.axis_index(HIDDEN)
    flags = jnp.stack([role, core, lax.axis_index("x")]).astype(jnp.int32)
    token_batch = token_rows[0]
    group_rows = token_batch.shape[0]
    slice_width = adapter_in.shape[1]
    cols = frozen_gate_up_weight.shape[2]
    token_part = lax.dynamic_slice_in_dim(token_batch, shard_index * slice_width, slice_width, 1)

    in_bf = adapter_in.astype(BF)
    out_bf = adapter_out.astype(BF)
    ranks = 2 * in_bf.shape[2]

    def to_rank(matrix):
        part = jnp.einsum("knq,rn->kqr", matrix, token_part, preferred_element_type=F32)
        return part.reshape(ranks, group_rows)

    reduced = plus_partner(to_rank(in_bf), "ylo", 1)
    row_weight = KEEP_RATE ** staleness.astype(F32)
    rows = rows_by_x(token_batch, cotangent, row_weight[:, None])
    rows, own_weight, own_down, reduced = lax.optimization_barrier(
        (rows, frozen_gate_up_weight, down_weight.T, reduced)
    )
    rows = exchange(rows, "x")

    other_half = swapped(own_weight, "role")
    other_down = swapped(own_down, "role")
    reduced = plus_partner(plus_partner(reduced, "zl", 1), "zl", 2)
    other_half, other_down, reduced = lax.optimization_barrier((other_half, other_down, reduced))
    weights = (own_weight, other_half, swapped(own_weight, "core"), swapped(other_half, "core"))
    reduced = plus_partner(reduced, "zh", 1)
    down_pair = jnp.stack([own_down, other_down])
    downs = (down_pair, swapped(down_pair, "core"))
    rows, reduced = lax.optimization_barrier((rows, reduced))
    pieces = exchange(partials(flags, rows, weights, downs), "x")
    reduced = plus_partner(reduced, "zh", 2).astype(BF)
    base, hidden_old, through_part, out_part = middle(flags, pieces, reduced, out_bf)

    down_first, _ = lax.optimization_barrier((down_pair, pieces))
    through = spread(through_part, NEAR)
    through, down_later = lax.optimization_barrier((through, down_first))
    same_core = [shifted(down_first, "x", 1)]
    same_core += [shifted(down_later, "x", step) for step in (2, 3)]

    through = spread(sum_first(through).astype(BF), "zh")
    through = sum_first(through).astype(BF)
    in_part = ADAPTER_SCALE * jnp.dot(through, token_part, preferred_element_type=F32)
    packed = jnp.concatenate([out_part, in_part.astype(BF)], axis=1)
    packed, same_core = lax.optimization_barrier((packed, same_core))
    grads = spread(packed, ALL_GROUPS)
    blocks = [down_pair, *same_core, downs[1], *(swapped(b, "core") for b in same_core)]
    old_parts = layer_call(old_kernel, group_rows, slice_width, blocks, flags, hidden_old)
    grads, old_parts = lax.optimization_barrier((grads, old_parts))
    grads = sum_first(grads)
    grad_in = grads[:, cols:].reshape(2, -1, slice_width).transpose(0, 2, 1)
    grad_out = grads[:, :cols].reshape(2, -1, cols)
    new_in, new_m_in, new_s_in = adam_update(adapter_in, grad_in, moment_in, square_in)
    new_out, new_m_out, new_s_out = adam_update(adapter_out, grad_out, moment_out, square_out)

    positions = jnp.arange(group_rows)
    live = jnp.logical_or(role == 0, positions < prefill_rows[0])

    def finish(total):
        total = total.astype(BF).T
        return jnp.where(live[:, None], total, jnp.zeros_like(total))

    old_parts = old_parts.reshape(4, 2, 4, slice_width, group_rows)
    side = lax.axis_index("ylo")
    give = swapped(lax.dynamic_index_in_dim(old_parts, 1 - side, 1, keepdims=False), "ylo")
    keep = lax.dynamic_index_in_dim(old_parts, side, 1, keepdims=False)
    pair = (keep.astype(F32) + give.astype(F32)).astype(BF)
    renewed = hidden_total(to_rank(new_in.astype(BF))).astype(BF)
    near_old = shifted_sum(pair, "zl")
    new_parts = layer_call(
        new_kernel, group_rows, slice_width, blocks, flags, base, renewed, new_out.astype(BF)
    )
    near_new = sum_first(exchange(new_parts.reshape(8, 4, slice_width, group_rows), NEAR))
    near = jnp.stack([near_old, near_new], axis=1).astype(BF)
    layers = sum_first(exchange(near, "zh"))
    layer_old, layer_new = finish(layers[0]), finish(layers[1])
    return (
        layer_old[None],
        layer_new[None],
        new_in[None],
        new_out[None],
        new_m_in[None],
        new_s_in[None],
        new_m_out[None],
        new_s_out[None],
    )


def solution(mesh):
    fine = Mesh(mesh.devices.reshape(2, 4, 2, 4, 4, 2), ("role", "x", "core", "zh", "zl", "ylo"))
    wide = ("role", "x", "core")
    in_specs = (
        P("role", DP, None),
        P(DP, None),
        P(DP),
        P(DP),
        P(None, wide, HIDDEN),
        P(HIDDEN, wide),
        P(None, HIDDEN, None),
        P(None, None, HIDDEN),
        P(None, HIDDEN, None),
        P(None, HIDDEN, None),
        P(None, None, HIDDEN),
        P(None, None, HIDDEN),
    )
    out_specs = (
        P("role", DP, HIDDEN),
        P("role", DP, HIDDEN),
        P("role", None, HIDDEN, None),
        P("role", None, None, HIDDEN),
        P("role", None, HIDDEN, None),
        P("role", None, HIDDEN, None),
        P("role", None, None, HIDDEN),
        P("role", None, None, HIDDEN),
    )
    return jax.shard_map(step, mesh=fine, in_specs=in_specs, out_specs=out_specs, check_vma=False)
```

```python
import jax
import jax.numpy as jnp
from jax import lax
from jax.experimental import pallas as pl
from jax.experimental.pallas import tpu as pltpu
from jax.sharding import Mesh
from jax.sharding import PartitionSpec as P


D = 5120
OPT_STEP = 10

ADAPTER_SCALE = 2.0
BETA_ONE = 0.9
BETA_TWO = 0.999
RATE_FACTOR = 0.34
ADAM_EPS = 1e-08
KEEP_RATE = 0.75

DP = ("x", "core")
NEAR = ("zl", "ylo")
HIDDEN = ("zh", "zl", "ylo")
BF = jnp.bfloat16
F32 = jnp.float32


VMEM = pl.BlockSpec(memory_space=pltpu.VMEM)
SMEM = pl.BlockSpec(memory_space=pltpu.SMEM)
ANY = pl.BlockSpec(memory_space=pl.ANY)


def exchange(pieces, axis):
    return lax.all_to_all(pieces, axis, split_axis=0, concat_axis=0, tiled=True)


def swapped(value, axis):
    return lax.ppermute(value, axis, [(0, 1), (1, 0)])


def spread(value, axis):
    count = lax.axis_size(axis)
    return exchange(jnp.broadcast_to(value, (count, *value.shape)), axis)


def sum_first(pieces):
    return pieces.astype(F32).sum(axis=0)


def shifted(value, axis, step):
    count = lax.axis_size(axis)
    return lax.ppermute(value, axis, [(i, (i + step) % count) for i in range(count)])


def plus_partner(value, axis, step):
    count = lax.axis_size(axis)
    return value + lax.ppermute(value, axis, [(i, i ^ step) for i in range(count)])


def shifted_sum(pieces, axis):
    index = lax.axis_index(axis)
    count = lax.axis_size(axis)
    total = lax.dynamic_index_in_dim(pieces, index, 0, keepdims=False).astype(F32)
    for step in range(1, count):
        piece = lax.dynamic_index_in_dim(pieces, lax.rem(index + step, count), 0, keepdims=False)
        total = total + shifted(piece, axis, step).astype(F32)
    return total


def adam_update(param, grad, first, second):
    learn_rate = RATE_FACTOR / D**0.5
    first_new = BETA_ONE * first + (1.0 - BETA_ONE) * grad
    second_new = BETA_TWO * second + (1.0 - BETA_TWO) * grad * grad
    first_fix = first_new / (1.0 - BETA_ONE**OPT_STEP)
    second_fix = second_new / (1.0 - BETA_TWO**OPT_STEP)
    return (
        param - learn_rate * first_fix / (jnp.sqrt(second_fix) + ADAM_EPS),
        first_new,
        second_new,
    )


def dot(a, b, dims):
    return lax.dot_general(a, b, (dims, ((), ())), preferred_element_type=F32)


def rows_kernel(token_ref, cotangent_ref, scale_ref, out_ref):
    width = out_ref.shape[4]
    scale = scale_ref[...]
    for half in range(2):
        for x in range(4):
            columns = slice((half * 4 + x) * width, (half * 4 + x + 1) * width)
            out_ref[x, 0, half] = token_ref[:, columns]
            out_ref[x, 1, half] = (scale * cotangent_ref[:, columns].astype(F32)).astype(BF)


def rows_by_x(tokens, cotangent, scale):
    group, width = tokens.shape
    return pl.pallas_call(
        rows_kernel,
        out_shape=jax.ShapeDtypeStruct((4, 2, 2, group, width // 8), BF),
        in_specs=[VMEM, VMEM, VMEM],
        out_specs=VMEM,
        name="rows_by_x",
    )(tokens, cotangent, scale)


def partial_kernel(flag_ref, rows_ref, *refs):
    weight_refs, down_refs = refs[:4], refs[4:6]
    out_ref, weight, down, held, in_sems, out_sems = refs[6:]
    role, core = flag_ref[0], flag_ref[1]
    depth = weight_refs[0].shape[1]
    weight_loads, down_loads = [], []
    for i in range(2):
        side = core if i == 0 else 1 - core
        place = pl.ds(pl.multiple_of(side * depth, depth), depth)
        for j in range(2):
            half = role if j == 0 else 1 - role
            n = 2 * i + j
            down_loads.append(pltpu.make_async_copy(down_refs[i].at[j], down.at[half, place, :], in_sems.at[n]))
            weight_loads.append(pltpu.make_async_copy(weight_refs[n], weight.at[half, :, place, :], in_sems.at[4 + n]))
    for copy in down_loads + weight_loads:
        copy.start()

    count, group = rows_ref.shape[0], rows_ref.shape[3]

    def all_rows(which, half):
        return jnp.concatenate([rows_ref[x, which, half] for x in range(count)], axis=0)

    stores = []
    for k in (2, 0, 1):
        for copy in {2: down_loads, 0: weight_loads, 1: []}[k]:
            copy.wait()
        total = 0.0
        for half in range(2):
            if k < 2:
                total += dot(all_rows(0, half), weight[half, k], ((1,), (0,)))
            else:
                total += dot(all_rows(1, half), down[half], ((1,), (0,)))
        turned = total.astype(BF).T
        for x in range(count):
            held[k, x] = turned[:, x * group : (x + 1) * group]
        copy = pltpu.make_async_copy(held.at[k], out_ref.at[:, k], out_sems.at[k])
        copy.start()
        stores.append(copy)
    for copy in stores:
        copy.wait()


def partials(flags, rows, weights, downs):
    count, _, _, group, _ = rows.shape
    _, depth, cols = weights[0].shape
    return pl.pallas_call(
        partial_kernel,
        out_shape=jax.ShapeDtypeStruct((count, 3, cols, group), BF),
        in_specs=[SMEM, VMEM] + [ANY] * 6,
        out_specs=ANY,
        scratch_shapes=[
            pltpu.VMEM((2, 2, 2 * depth, cols), BF),
            pltpu.VMEM((2, 2 * depth, cols), BF),
            pltpu.VMEM((3, count, cols, group), BF),
            pltpu.SemaphoreType.DMA((8,)),
            pltpu.SemaphoreType.DMA((3,)),
        ],
        name="partials",
    )(flags, rows, *weights, *downs)


def middle_kernel(flag_ref, pieces_ref, reduced_ref, lift_ref, base_ref, hidden_ref, through_ref, grad_ref):
    total = [pieces_ref[0, k].astype(F32) for k in range(3)]
    for x in range(1, pieces_ref.shape[0]):
        for k in range(3):
            total[k] = total[k] + pieces_ref[x, k].astype(F32)
    rank = lift_ref.shape[1]
    pre = []
    for k in range(2):
        base_ref[k] = total[k]
        part = reduced_ref[k * rank : (k + 1) * rank, :]
        pre.append(total[k] + ADAPTER_SCALE * dot(lift_ref[k], part, ((0,), (0,))))
    gate, up = pre
    sigma = jax.nn.sigmoid(gate)
    silu = gate * sigma
    hidden_ref[...] = (silu * up).astype(BF)
    grad_hidden = jnp.where(flag_ref[0] == 0, total[2], jnp.zeros_like(total[2]))
    grads = (
        (grad_hidden * up * sigma * (1.0 + gate * (1.0 - sigma))).astype(BF),
        (grad_hidden * silu).astype(BF),
    )
    for k in range(2):
        block = slice(k * rank, (k + 1) * rank)
        through_ref[block, :] = dot(lift_ref[k], grads[k], ((1,), (0,))).astype(BF)
        grad_ref[block, :] = (
            ADAPTER_SCALE * dot(reduced_ref[block, :], grads[k], ((1,), (1,)))
        ).astype(BF)


def middle(flags, pieces, reduced, lift):
    _, _, cols, group = pieces.shape
    ranks = reduced.shape[0]
    return pl.pallas_call(
        middle_kernel,
        out_shape=(
            jax.ShapeDtypeStruct((2, cols, group), F32),
            jax.ShapeDtypeStruct((cols, group), BF),
            jax.ShapeDtypeStruct((ranks, group), BF),
            jax.ShapeDtypeStruct((ranks, cols), BF),
        ),
        in_specs=[SMEM, VMEM, VMEM, VMEM],
        out_specs=(VMEM, VMEM, VMEM, VMEM),
        name="middle",
    )(flags, pieces, reduced, lift)


def down_product(flag_ref, hidden, block_refs, out_ref):
    role, x, core = flag_ref[0], flag_ref[2], flag_ref[1]
    size = out_ref.shape[1]
    for i in range(2):
        side = core if i == 0 else 1 - core
        for step in range(4):
            source = lax.rem(x + 4 - step, 4)
            for j in range(2):
                half = role if j == 0 else 1 - role
                product = dot(block_refs[4 * i + step][j], hidden, ((1,), (0,))).astype(BF)
                block = half * 8 + 2 * source + side
                for s in range(2):
                    place = 2 * block + s
                    out_ref[lax.rem(place, 8) * 4 + lax.div(place, 8)] = product[s * size : (s + 1) * size]


def old_kernel(flag_ref, hidden_ref, *refs):
    down_product(flag_ref, hidden_ref[...], refs[:-1], refs[-1])


def new_kernel(flag_ref, base_ref, reduced_ref, lift_ref, *refs):
    rank = lift_ref.shape[1]
    post = []
    for k in range(2):
        part = reduced_ref[k * rank : (k + 1) * rank, :]
        post.append(base_ref[k] + ADAPTER_SCALE * dot(lift_ref[k], part, ((0,), (0,))))
    hidden = (post[0] * jax.nn.sigmoid(post[0]) * post[1]).astype(BF)
    down_product(flag_ref, hidden, refs[:-1], refs[-1])


def layer_call(kernel, group, width, blocks, *operands):
    return pl.pallas_call(
        kernel,
        out_shape=jax.ShapeDtypeStruct((32, width, group), BF),
        in_specs=[SMEM] + [VMEM] * (len(operands) - 1 + len(blocks)),
        out_specs=VMEM,
    )(*operands, *blocks)


def step(
    token_rows,
    cotangent,
    staleness,
    prefill_rows,
    frozen_gate_up_weight,
    down_weight,
    adapter_in,
    adapter_out,
    moment_in,
    square_in,
    moment_out,
    square_out,
):
    role = lax.axis_index("role")
    core = lax.axis_index("core")
    shard_index = lax.axis_index(HIDDEN)
    flags = jnp.stack([role, core, lax.axis_index("x")]).astype(jnp.int32)
    token_batch = token_rows[0]
    group_rows = token_batch.shape[0]
    slice_width = adapter_in.shape[1]
    cols = frozen_gate_up_weight.shape[2]
    token_part = lax.dynamic_slice_in_dim(token_batch, shard_index * slice_width, slice_width, 1)

    in_bf = adapter_in.astype(BF)
    out_bf = adapter_out.astype(BF)
    ranks = 2 * in_bf.shape[2]

    def to_rank(matrix):
        part = jnp.einsum("knq,rn->kqr", matrix, token_part, preferred_element_type=F32)
        return part.reshape(ranks, group_rows)

    reduced = plus_partner(to_rank(in_bf), "ylo", 1)
    row_weight = KEEP_RATE ** staleness.astype(F32)
    rows = rows_by_x(token_batch, cotangent, row_weight[:, None])
    rows = exchange(rows, "x")
    own_weight, own_down, reduced = lax.optimization_barrier((frozen_gate_up_weight, down_weight.T, reduced))

    other_half = swapped(own_weight, "role")
    other_down = swapped(own_down, "role")
    reduced = plus_partner(plus_partner(reduced, "zl", 1), "zl", 2)
    other_half, other_down, reduced = lax.optimization_barrier((other_half, other_down, reduced))
    weights = (own_weight, other_half, swapped(own_weight, "core"), swapped(other_half, "core"))
    down_pair = jnp.stack([own_down, other_down])
    downs = (down_pair, swapped(down_pair, "core"))
    rows, reduced = lax.optimization_barrier((rows, reduced))
    pieces = exchange(partials(flags, rows, weights, downs), "x")
    reduced = plus_partner(plus_partner(reduced, "zh", 1), "zh", 2).astype(BF)
    base, hidden_old, through_part, out_part = middle(flags, pieces, reduced, out_bf)

    down_first, _ = lax.optimization_barrier((down_pair, pieces))
    through = sum_first(spread(through_part, NEAR)).astype(BF)
    through = spread(through, "zh")
    through = sum_first(through).astype(BF)
    behind, ahead = shifted(down_first, "x", 1), shifted(down_first, "x", 3)
    across = jnp.stack([shifted(behind[0], "x", 1), shifted(ahead[1], "x", 3)])
    same_core = [behind, across, ahead]

    def to_both_halves(value):
        return value + lax.ppermute(value, "role", [(0, 1)])

    out_part = to_both_halves(out_part)
    in_part = ADAPTER_SCALE * jnp.dot(through, token_part, preferred_element_type=F32)
    in_part = to_both_halves(in_part.astype(BF))
    other_behind, other_ahead = swapped(behind, "core"), swapped(ahead, "core")
    packed = jnp.concatenate([out_part, in_part], axis=1)
    packed, same_core = lax.optimization_barrier((packed, same_core))
    grads = spread(packed, DP)
    other_across = swapped(same_core[1], "core")
    blocks = [down_pair, *same_core, downs[1], other_behind, other_across, other_ahead]
    old_parts = layer_call(old_kernel, group_rows, slice_width, blocks, flags, hidden_old)
    grads, old_parts = lax.optimization_barrier((grads, old_parts))
    grads = sum_first(grads)
    grad_in = grads[:, cols:].reshape(2, -1, slice_width).transpose(0, 2, 1)
    grad_out = grads[:, :cols].reshape(2, -1, cols)
    new_in, new_m_in, new_s_in = adam_update(adapter_in, grad_in, moment_in, square_in)
    new_out, new_m_out, new_s_out = adam_update(adapter_out, grad_out, moment_out, square_out)

    positions = jnp.arange(group_rows)
    live = jnp.logical_or(role == 0, positions < prefill_rows[0])

    def finish(total):
        total = total.astype(BF).T
        return jnp.where(live[:, None], total, jnp.zeros_like(total))

    old_parts = old_parts.reshape(4, 2, 4, slice_width, group_rows)
    side = lax.axis_index("ylo")
    give = swapped(lax.dynamic_index_in_dim(old_parts, 1 - side, 1, keepdims=False), "ylo")
    keep = lax.dynamic_index_in_dim(old_parts, side, 1, keepdims=False)
    pair = (keep.astype(F32) + give.astype(F32)).astype(BF)
    renewed = to_rank(new_in.astype(BF)).astype(BF)
    renewed = spread(renewed, NEAR)
    renewed = sum_first(spread(sum_first(renewed).astype(BF), "zh")).astype(BF)
    near_old = shifted_sum(pair, "zl")
    new_parts = layer_call(new_kernel, group_rows, slice_width, blocks, flags, base, renewed, new_out.astype(BF))
    near_new = sum_first(exchange(new_parts.reshape(8, 4, slice_width, group_rows), NEAR))
    near = jnp.stack([near_old, near_new], axis=1).astype(BF)
    layers = sum_first(exchange(near, "zh"))
    layer_old, layer_new = finish(layers[0]), finish(layers[1])
    return (
        layer_old[None],
        layer_new[None],
        new_in[None],
        new_out[None],
        new_m_in[None],
        new_s_in[None],
        new_m_out[None],
        new_s_out[None],
    )


def solution(mesh):
    fine = Mesh(mesh.devices.reshape(2, 4, 2, 4, 4, 2), ("role", "x", "core", "zh", "zl", "ylo"))
    wide = ("role", "x", "core")
    in_specs = (
        P("role", DP, None),
        P(DP, None),
        P(DP),
        P(DP),
        P(None, wide, HIDDEN),
        P(HIDDEN, wide),
        P(None, HIDDEN, None),
        P(None, None, HIDDEN),
        P(None, HIDDEN, None),
        P(None, HIDDEN, None),
        P(None, None, HIDDEN),
        P(None, None, HIDDEN),
    )
    out_specs = (
        P("role", DP, HIDDEN),
        P("role", DP, HIDDEN),
        P("role", None, HIDDEN, None),
        P("role", None, None, HIDDEN),
        P("role", None, HIDDEN, None),
        P("role", None, HIDDEN, None),
        P("role", None, None, HIDDEN),
        P("role", None, None, HIDDEN),
    )
    return jax.shard_map(step, mesh=fine, in_specs=in_specs, out_specs=out_specs, check_vma=False)
```

```python
import jax
import jax.numpy as jnp
from jax import lax
from jax.experimental import pallas as pl
from jax.experimental.pallas import tpu as pltpu
from jax.sharding import Mesh
from jax.sharding import PartitionSpec as P


D = 5120
OPT_STEP = 10

ADAPTER_SCALE = 2.0
BETA_ONE = 0.9
BETA_TWO = 0.999
RATE_FACTOR = 0.34
ADAM_EPS = 1e-08
KEEP_RATE = 0.75

DP = ("x", "core")
NEAR = ("zl", "ylo")
HIDDEN = ("zh", "zl", "ylo")
BF = jnp.bfloat16
F32 = jnp.float32


VMEM = pl.BlockSpec(memory_space=pltpu.VMEM)
SMEM = pl.BlockSpec(memory_space=pltpu.SMEM)
ANY = pl.BlockSpec(memory_space=pl.ANY)


def exchange(pieces, axis):
    return lax.all_to_all(pieces, axis, split_axis=0, concat_axis=0, tiled=True)


def swapped(value, axis):
    return lax.ppermute(value, axis, [(0, 1), (1, 0)])


def spread(value, axis):
    count = lax.axis_size(axis)
    return exchange(jnp.broadcast_to(value, (count, *value.shape)), axis)


def sum_first(pieces):
    return pieces.astype(F32).sum(axis=0)


def shifted(value, axis, step):
    count = lax.axis_size(axis)
    return lax.ppermute(value, axis, [(i, (i + step) % count) for i in range(count)])


def plus_partner(value, axis, step):
    count = lax.axis_size(axis)
    return value + lax.ppermute(value, axis, [(i, i ^ step) for i in range(count)])


def halved(pieces, axis, bit):
    mine = lax.axis_index(axis)
    if bit == 1:
        both = pieces.reshape(2, 2, *pieces.shape[1:])
        mine, dim = lax.rem(mine, 2), 1
    else:
        both = pieces
        mine, dim = lax.div(mine, 2), 0
    keep = lax.dynamic_index_in_dim(both, mine, dim, keepdims=False)
    give = lax.dynamic_index_in_dim(both, 1 - mine, dim, keepdims=False)
    got = lax.ppermute(give, axis, [(i, i ^ bit) for i in range(4)])
    return (keep.astype(F32) + got.astype(F32)).astype(BF)


def adam_update(param, grad, first, second):
    learn_rate = RATE_FACTOR / D**0.5
    first_new = BETA_ONE * first + (1.0 - BETA_ONE) * grad
    second_new = BETA_TWO * second + (1.0 - BETA_TWO) * grad * grad
    first_fix = first_new / (1.0 - BETA_ONE**OPT_STEP)
    second_fix = second_new / (1.0 - BETA_TWO**OPT_STEP)
    return (
        param - learn_rate * first_fix / (jnp.sqrt(second_fix) + ADAM_EPS),
        first_new,
        second_new,
    )


def dot(a, b, dims):
    return lax.dot_general(a, b, (dims, ((), ())), preferred_element_type=F32)


def rows_kernel(token_ref, cotangent_ref, scale_ref, out_ref):
    width = out_ref.shape[4]
    scale = scale_ref[...]
    for half in range(2):
        for x in range(4):
            columns = slice((half * 4 + x) * width, (half * 4 + x + 1) * width)
            out_ref[x, 0, half] = token_ref[:, columns]
            out_ref[x, 1, half] = (scale * cotangent_ref[:, columns].astype(F32)).astype(BF)


def rows_by_x(tokens, cotangent, scale):
    group, width = tokens.shape
    return pl.pallas_call(
        rows_kernel,
        out_shape=jax.ShapeDtypeStruct((4, 2, 2, group, width // 8), BF),
        in_specs=[VMEM, VMEM, VMEM],
        out_specs=VMEM,
        name="rows_by_x",
    )(tokens, cotangent, scale)


def partial_kernel(flag_ref, rows_ref, *refs):
    weight_refs, down_refs = refs[:4], refs[4:6]
    out_ref, weight, down, held, in_sems, out_sems = refs[6:]
    role, core = flag_ref[0], flag_ref[1]
    depth = weight_refs[0].shape[1]
    weight_loads, down_loads = [], []
    for i in range(2):
        side = core if i == 0 else 1 - core
        place = pl.ds(pl.multiple_of(side * depth, depth), depth)
        for j in range(2):
            half = role if j == 0 else 1 - role
            n = 2 * i + j
            down_loads.append(pltpu.make_async_copy(down_refs[i].at[j], down.at[half, place, :], in_sems.at[n]))
            weight_loads.append(pltpu.make_async_copy(weight_refs[n], weight.at[half, :, place, :], in_sems.at[4 + n]))
    for copy in down_loads + weight_loads:
        copy.start()

    count, group = rows_ref.shape[0], rows_ref.shape[3]

    def all_rows(which, half):
        return jnp.concatenate([rows_ref[x, which, half] for x in range(count)], axis=0)

    stores = []
    for k in (2, 0, 1):
        for copy in {2: down_loads, 0: weight_loads, 1: []}[k]:
            copy.wait()
        total = 0.0
        for half in range(2):
            if k < 2:
                total += dot(all_rows(0, half), weight[half, k], ((1,), (0,)))
            else:
                total += dot(all_rows(1, half), down[half], ((1,), (0,)))
        turned = total.astype(BF).T
        for x in range(count):
            held[k, x] = turned[:, x * group : (x + 1) * group]
        copy = pltpu.make_async_copy(held.at[k], out_ref.at[:, k], out_sems.at[k])
        copy.start()
        stores.append(copy)
    for copy in stores:
        copy.wait()


def partials(flags, rows, weights, downs):
    count, _, _, group, _ = rows.shape
    _, depth, cols = weights[0].shape
    return pl.pallas_call(
        partial_kernel,
        out_shape=jax.ShapeDtypeStruct((count, 3, cols, group), BF),
        in_specs=[SMEM, VMEM] + [ANY] * 6,
        out_specs=ANY,
        scratch_shapes=[
            pltpu.VMEM((2, 2, 2 * depth, cols), BF),
            pltpu.VMEM((2, 2 * depth, cols), BF),
            pltpu.VMEM((3, count, cols, group), BF),
            pltpu.SemaphoreType.DMA((8,)),
            pltpu.SemaphoreType.DMA((3,)),
        ],
        name="partials",
    )(flags, rows, *weights, *downs)


def middle_kernel(flag_ref, pieces_ref, reduced_ref, lift_ref, base_ref, hidden_ref, through_ref, grad_ref):
    total = [pieces_ref[0, k].astype(F32) for k in range(3)]
    for x in range(1, pieces_ref.shape[0]):
        for k in range(3):
            total[k] = total[k] + pieces_ref[x, k].astype(F32)
    rank = lift_ref.shape[1]
    pre = []
    for k in range(2):
        base_ref[k] = total[k]
        part = reduced_ref[k * rank : (k + 1) * rank, :]
        pre.append(total[k] + ADAPTER_SCALE * dot(lift_ref[k], part, ((0,), (0,))))
    gate, up = pre
    sigma = jax.nn.sigmoid(gate)
    silu = gate * sigma
    hidden_ref[...] = (silu * up).astype(BF)
    grad_hidden = jnp.where(flag_ref[0] == 0, total[2], jnp.zeros_like(total[2]))
    grads = (
        (grad_hidden * up * sigma * (1.0 + gate * (1.0 - sigma))).astype(BF),
        (grad_hidden * silu).astype(BF),
    )
    for k in range(2):
        block = slice(k * rank, (k + 1) * rank)
        through_ref[block, :] = dot(lift_ref[k], grads[k], ((1,), (0,))).astype(BF)
        grad_ref[block, :] = (
            ADAPTER_SCALE * dot(reduced_ref[block, :], grads[k], ((1,), (1,)))
        ).astype(BF)


def middle(flags, pieces, reduced, lift):
    _, _, cols, group = pieces.shape
    ranks = reduced.shape[0]
    return pl.pallas_call(
        middle_kernel,
        out_shape=(
            jax.ShapeDtypeStruct((2, cols, group), F32),
            jax.ShapeDtypeStruct((cols, group), BF),
            jax.ShapeDtypeStruct((ranks, group), BF),
            jax.ShapeDtypeStruct((ranks, cols), BF),
        ),
        in_specs=[SMEM, VMEM, VMEM, VMEM],
        out_specs=(VMEM, VMEM, VMEM, VMEM),
        name="middle",
    )(flags, pieces, reduced, lift)


def down_product(flag_ref, hidden, block_refs, out_ref):
    role, x, core = flag_ref[0], flag_ref[2], flag_ref[1]
    size = out_ref.shape[1]
    for i in range(2):
        side = core if i == 0 else 1 - core
        for step in range(4):
            source = lax.rem(x + 4 - step, 4)
            for j in range(2):
                half = role if j == 0 else 1 - role
                product = dot(block_refs[4 * i + step][j], hidden, ((1,), (0,))).astype(BF)
                block = half * 8 + 2 * source + side
                for s in range(2):
                    place = 2 * block + s
                    out_ref[lax.rem(place, 8) * 4 + lax.div(place, 8)] = product[s * size : (s + 1) * size]


def old_kernel(flag_ref, hidden_ref, *refs):
    down_product(flag_ref, hidden_ref[...], refs[:-1], refs[-1])


def new_kernel(flag_ref, base_ref, reduced_ref, lift_ref, *refs):
    rank = lift_ref.shape[1]
    post = []
    for k in range(2):
        part = reduced_ref[k * rank : (k + 1) * rank, :]
        post.append(base_ref[k] + ADAPTER_SCALE * dot(lift_ref[k], part, ((0,), (0,))))
    hidden = (post[0] * jax.nn.sigmoid(post[0]) * post[1]).astype(BF)
    down_product(flag_ref, hidden, refs[:-1], refs[-1])


def layer_call(kernel, group, width, blocks, *operands):
    return pl.pallas_call(
        kernel,
        out_shape=jax.ShapeDtypeStruct((32, width, group), BF),
        in_specs=[SMEM] + [VMEM] * (len(operands) - 1 + len(blocks)),
        out_specs=VMEM,
    )(*operands, *blocks)


def step(
    token_rows,
    cotangent,
    staleness,
    prefill_rows,
    frozen_gate_up_weight,
    down_weight,
    adapter_in,
    adapter_out,
    moment_in,
    square_in,
    moment_out,
    square_out,
):
    role = lax.axis_index("role")
    core = lax.axis_index("core")
    shard_index = lax.axis_index(HIDDEN)
    flags = jnp.stack([role, core, lax.axis_index("x")]).astype(jnp.int32)
    token_batch = token_rows[0]
    group_rows = token_batch.shape[0]
    slice_width = adapter_in.shape[1]
    cols = frozen_gate_up_weight.shape[2]
    token_part = lax.dynamic_slice_in_dim(token_batch, shard_index * slice_width, slice_width, 1)

    in_bf = adapter_in.astype(BF)
    out_bf = adapter_out.astype(BF)
    ranks = 2 * in_bf.shape[2]

    def to_rank(matrix):
        part = jnp.einsum("knq,rn->kqr", matrix, token_part, preferred_element_type=F32)
        return part.reshape(ranks, group_rows)

    reduced = plus_partner(to_rank(in_bf), "ylo", 1)
    row_weight = KEEP_RATE ** staleness.astype(F32)
    rows = rows_by_x(token_batch, cotangent, row_weight[:, None])
    rows = exchange(rows, "x")
    own_weight, own_down, reduced = lax.optimization_barrier((frozen_gate_up_weight, down_weight.T, reduced))

    other_half = swapped(own_weight, "role")
    other_down = swapped(own_down, "role")
    reduced = plus_partner(plus_partner(reduced, "zl", 1), "zl", 2)
    other_half, other_down, reduced = lax.optimization_barrier((other_half, other_down, reduced))
    weights = (own_weight, other_half, swapped(own_weight, "core"), swapped(other_half, "core"))
    down_pair = jnp.stack([own_down, other_down])
    downs = (down_pair, swapped(down_pair, "core"))
    rows, reduced = lax.optimization_barrier((rows, reduced))
    pieces = exchange(partials(flags, rows, weights, downs), "x")
    reduced = plus_partner(plus_partner(reduced, "zh", 1), "zh", 2).astype(BF)
    base, hidden_old, through_part, out_part = middle(flags, pieces, reduced, out_bf)

    down_first, _ = lax.optimization_barrier((down_pair, pieces))
    through = sum_first(spread(through_part, NEAR)).astype(BF)
    through = spread(through, "zh")
    through = sum_first(through).astype(BF)
    behind, ahead = shifted(down_first, "x", 1), shifted(down_first, "x", 3)
    across = shifted(behind, "x", 1)
    same_core = [behind, across, ahead]

    in_part = ADAPTER_SCALE * jnp.dot(through, token_part, preferred_element_type=F32)
    packed = jnp.concatenate([out_part, in_part.astype(BF)], axis=1)
    packed = packed + lax.ppermute(packed, "role", [(0, 1)])
    packed, same_core = lax.optimization_barrier((packed, same_core))
    grads = spread(packed, DP)
    other_core = [swapped(b, "core") for b in same_core]
    blocks = [down_pair, *same_core, downs[1], *other_core]
    old_parts = layer_call(old_kernel, group_rows, slice_width, blocks, flags, hidden_old)
    grads, old_parts = lax.optimization_barrier((grads, old_parts))
    grads = sum_first(grads)
    grad_in = grads[:, cols:].reshape(2, -1, slice_width).transpose(0, 2, 1)
    grad_out = grads[:, :cols].reshape(2, -1, cols)
    new_in, new_m_in, new_s_in = adam_update(adapter_in, grad_in, moment_in, square_in)
    new_out, new_m_out, new_s_out = adam_update(adapter_out, grad_out, moment_out, square_out)

    positions = jnp.arange(group_rows)
    live = jnp.logical_or(role == 0, positions < prefill_rows[0])

    def finish(total):
        total = total.T
        return jnp.where(live[:, None], total, jnp.zeros_like(total))

    old_parts = old_parts.reshape(4, 2, 4, slice_width, group_rows)
    side = lax.axis_index("ylo")
    give = swapped(lax.dynamic_index_in_dim(old_parts, 1 - side, 1, keepdims=False), "ylo")
    keep = lax.dynamic_index_in_dim(old_parts, side, 1, keepdims=False)
    pair = (keep.astype(F32) + give.astype(F32)).astype(BF)
    renewed = to_rank(new_in.astype(BF)).astype(BF)
    renewed = spread(renewed, NEAR)
    renewed = sum_first(spread(sum_first(renewed).astype(BF), "zh")).astype(BF)
    total_old = halved(pair, "zl", 1)
    new_parts = layer_call(new_kernel, group_rows, slice_width, blocks, flags, base, renewed, new_out.astype(BF))
    near_new = exchange(new_parts.reshape(8, 4, slice_width, group_rows), NEAR)
    total_old = halved(halved(halved(total_old, "zl", 2), "zh", 1), "zh", 2)
    total_new = sum_first(exchange(sum_first(near_new).astype(BF), "zh")).astype(BF)
    layer_old, layer_new = finish(total_old), finish(total_new)
    return (
        layer_old[None],
        layer_new[None],
        new_in[None],
        new_out[None],
        new_m_in[None],
        new_s_in[None],
        new_m_out[None],
        new_s_out[None],
    )


def solution(mesh):
    fine = Mesh(mesh.devices.reshape(2, 4, 2, 4, 4, 2), ("role", "x", "core", "zh", "zl", "ylo"))
    wide = ("role", "x", "core")
    in_specs = (
        P("role", DP, None),
        P(DP, None),
        P(DP),
        P(DP),
        P(None, wide, HIDDEN),
        P(HIDDEN, wide),
        P(None, HIDDEN, None),
        P(None, None, HIDDEN),
        P(None, HIDDEN, None),
        P(None, HIDDEN, None),
        P(None, None, HIDDEN),
        P(None, None, HIDDEN),
    )
    out_specs = (
        P("role", DP, HIDDEN),
        P("role", DP, HIDDEN),
        P("role", None, HIDDEN, None),
        P("role", None, None, HIDDEN),
        P("role", None, HIDDEN, None),
        P("role", None, HIDDEN, None),
        P("role", None, None, HIDDEN),
        P("role", None, None, HIDDEN),
    )
    return jax.shard_map(step, mesh=fine, in_specs=in_specs, out_specs=out_specs, check_vma=False)
```

```python
import jax
import jax.numpy as jnp
from jax import lax
from jax.experimental import pallas as pl
from jax.experimental.pallas import tpu as pltpu
from jax.sharding import Mesh
from jax.sharding import PartitionSpec as P


D = 5120
OPT_STEP = 10

ADAPTER_SCALE = 2.0
BETA_ONE = 0.9
BETA_TWO = 0.999
RATE_FACTOR = 0.34
ADAM_EPS = 1e-08
KEEP_RATE = 0.75

DP = ("x", "core")
NEAR = ("zl", "ylo")
HIDDEN = ("zh", "zl", "ylo")
BF = jnp.bfloat16
F32 = jnp.float32


VMEM = pl.BlockSpec(memory_space=pltpu.VMEM)
SMEM = pl.BlockSpec(memory_space=pltpu.SMEM)
ANY = pl.BlockSpec(memory_space=pl.ANY)


def exchange(pieces, axis):
    return lax.all_to_all(pieces, axis, split_axis=0, concat_axis=0, tiled=True)


def swapped(value, axis):
    return lax.ppermute(value, axis, [(0, 1), (1, 0)])


def spread(value, axis):
    count = lax.axis_size(axis)
    return exchange(jnp.broadcast_to(value, (count, *value.shape)), axis)


def sum_first(pieces):
    return pieces.astype(F32).sum(axis=0)


def shifted(value, axis, step):
    count = lax.axis_size(axis)
    return lax.ppermute(value, axis, [(i, (i + step) % count) for i in range(count)])


def plus_partner(value, axis, step):
    count = lax.axis_size(axis)
    return value + lax.ppermute(value, axis, [(i, i ^ step) for i in range(count)])


def shifted_sum(pieces, axis):
    index = lax.axis_index(axis)
    count = lax.axis_size(axis)
    total = lax.dynamic_index_in_dim(pieces, index, 0, keepdims=False).astype(F32)
    for step in range(1, count):
        piece = lax.dynamic_index_in_dim(pieces, lax.rem(index + step, count), 0, keepdims=False)
        total = total + shifted(piece, axis, step).astype(F32)
    return total


def adam_update(param, grad, first, second):
    learn_rate = RATE_FACTOR / D**0.5
    first_new = BETA_ONE * first + (1.0 - BETA_ONE) * grad
    second_new = BETA_TWO * second + (1.0 - BETA_TWO) * grad * grad
    first_fix = first_new / (1.0 - BETA_ONE**OPT_STEP)
    second_fix = second_new / (1.0 - BETA_TWO**OPT_STEP)
    return (
        param - learn_rate * first_fix / (jnp.sqrt(second_fix) + ADAM_EPS),
        first_new,
        second_new,
    )


def dot(a, b, dims):
    return lax.dot_general(a, b, (dims, ((), ())), preferred_element_type=F32)


def rows_kernel(token_ref, cotangent_ref, scale_ref, out_ref):
    width = out_ref.shape[4]
    scale = scale_ref[...]
    for half in range(2):
        for x in range(4):
            columns = slice((half * 4 + x) * width, (half * 4 + x + 1) * width)
            out_ref[x, 0, half] = token_ref[:, columns]
            out_ref[x, 1, half] = (scale * cotangent_ref[:, columns].astype(F32)).astype(BF)


def rows_by_x(tokens, cotangent, scale):
    group, width = tokens.shape
    return pl.pallas_call(
        rows_kernel,
        out_shape=jax.ShapeDtypeStruct((4, 2, 2, group, width // 8), BF),
        in_specs=[VMEM, VMEM, VMEM],
        out_specs=VMEM,
        name="rows_by_x",
    )(tokens, cotangent, scale)


def partial_kernel(flag_ref, rows_ref, *refs):
    weight_refs, down_refs = refs[:4], refs[4:6]
    out_ref, weight, down, held, in_sems, out_sems = refs[6:]
    role, core = flag_ref[0], flag_ref[1]
    depth = weight_refs[0].shape[1]
    weight_loads, down_loads = [], []
    for i in range(2):
        side = core if i == 0 else 1 - core
        place = pl.ds(pl.multiple_of(side * depth, depth), depth)
        for j in range(2):
            half = role if j == 0 else 1 - role
            n = 2 * i + j
            down_loads.append(pltpu.make_async_copy(down_refs[i].at[j], down.at[half, place, :], in_sems.at[n]))
            weight_loads.append(pltpu.make_async_copy(weight_refs[n], weight.at[half, :, place, :], in_sems.at[4 + n]))
    for copy in down_loads + weight_loads:
        copy.start()

    count, group = rows_ref.shape[0], rows_ref.shape[3]

    def all_rows(which, half):
        return jnp.concatenate([rows_ref[x, which, half] for x in range(count)], axis=0)

    stores = []
    for k in (2, 0, 1):
        for copy in {2: down_loads, 0: weight_loads, 1: []}[k]:
            copy.wait()
        total = 0.0
        for half in range(2):
            if k < 2:
                total += dot(all_rows(0, half), weight[half, k], ((1,), (0,)))
            else:
                total += dot(all_rows(1, half), down[half], ((1,), (0,)))
        turned = total.astype(BF).T
        for x in range(count):
            held[k, x] = turned[:, x * group : (x + 1) * group]
        copy = pltpu.make_async_copy(held.at[k], out_ref.at[:, k], out_sems.at[k])
        copy.start()
        stores.append(copy)
    for copy in stores:
        copy.wait()


def partials(flags, rows, weights, downs):
    count, _, _, group, _ = rows.shape
    _, depth, cols = weights[0].shape
    return pl.pallas_call(
        partial_kernel,
        out_shape=jax.ShapeDtypeStruct((count, 3, cols, group), BF),
        in_specs=[SMEM, VMEM] + [ANY] * 6,
        out_specs=ANY,
        scratch_shapes=[
            pltpu.VMEM((2, 2, 2 * depth, cols), BF),
            pltpu.VMEM((2, 2 * depth, cols), BF),
            pltpu.VMEM((3, count, cols, group), BF),
            pltpu.SemaphoreType.DMA((8,)),
            pltpu.SemaphoreType.DMA((3,)),
        ],
        name="partials",
    )(flags, rows, *weights, *downs)


def middle_kernel(flag_ref, pieces_ref, reduced_ref, lift_ref, base_ref, hidden_ref, through_ref, grad_ref):
    total = [pieces_ref[0, k].astype(F32) for k in range(3)]
    for x in range(1, pieces_ref.shape[0]):
        for k in range(3):
            total[k] = total[k] + pieces_ref[x, k].astype(F32)
    rank = lift_ref.shape[1]
    pre = []
    for k in range(2):
        base_ref[k] = total[k]
        part = reduced_ref[k * rank : (k + 1) * rank, :]
        pre.append(total[k] + ADAPTER_SCALE * dot(lift_ref[k], part, ((0,), (0,))))
    gate, up = pre
    sigma = jax.nn.sigmoid(gate)
    silu = gate * sigma
    hidden_ref[...] = (silu * up).astype(BF)
    grad_hidden = jnp.where(flag_ref[0] == 0, total[2], jnp.zeros_like(total[2]))
    grads = (
        (grad_hidden * up * sigma * (1.0 + gate * (1.0 - sigma))).astype(BF),
        (grad_hidden * silu).astype(BF),
    )
    for k in range(2):
        block = slice(k * rank, (k + 1) * rank)
        through_ref[block, :] = dot(lift_ref[k], grads[k], ((1,), (0,))).astype(BF)
        grad_ref[block, :] = (
            ADAPTER_SCALE * dot(reduced_ref[block, :], grads[k], ((1,), (1,)))
        ).astype(BF)


def middle(flags, pieces, reduced, lift):
    _, _, cols, group = pieces.shape
    ranks = reduced.shape[0]
    return pl.pallas_call(
        middle_kernel,
        out_shape=(
            jax.ShapeDtypeStruct((2, cols, group), F32),
            jax.ShapeDtypeStruct((cols, group), BF),
            jax.ShapeDtypeStruct((ranks, group), BF),
            jax.ShapeDtypeStruct((ranks, cols), BF),
        ),
        in_specs=[SMEM, VMEM, VMEM, VMEM],
        out_specs=(VMEM, VMEM, VMEM, VMEM),
        name="middle",
    )(flags, pieces, reduced, lift)


def down_product(flag_ref, hidden, block_refs, out_ref):
    role, x, core = flag_ref[0], flag_ref[2], flag_ref[1]
    size = out_ref.shape[1]
    for i in range(2):
        side = core if i == 0 else 1 - core
        for step in range(4):
            source = lax.rem(x + 4 - step, 4)
            for j in range(2):
                half = role if j == 0 else 1 - role
                product = dot(block_refs[4 * i + step][j], hidden, ((1,), (0,))).astype(BF)
                block = half * 8 + 2 * source + side
                for s in range(2):
                    place = 2 * block + s
                    out_ref[lax.rem(place, 8) * 4 + lax.div(place, 8)] = product[s * size : (s + 1) * size]


def old_kernel(flag_ref, hidden_ref, *refs):
    down_product(flag_ref, hidden_ref[...], refs[:-1], refs[-1])


def new_kernel(flag_ref, base_ref, reduced_ref, lift_ref, *refs):
    rank = lift_ref.shape[1]
    post = []
    for k in range(2):
        part = reduced_ref[k * rank : (k + 1) * rank, :]
        post.append(base_ref[k] + ADAPTER_SCALE * dot(lift_ref[k], part, ((0,), (0,))))
    hidden = (post[0] * jax.nn.sigmoid(post[0]) * post[1]).astype(BF)
    down_product(flag_ref, hidden, refs[:-1], refs[-1])


def layer_call(kernel, group, width, blocks, *operands):
    return pl.pallas_call(
        kernel,
        out_shape=jax.ShapeDtypeStruct((32, width, group), BF),
        in_specs=[SMEM] + [VMEM] * (len(operands) - 1 + len(blocks)),
        out_specs=VMEM,
    )(*operands, *blocks)


def step(
    token_rows,
    cotangent,
    staleness,
    prefill_rows,
    frozen_gate_up_weight,
    down_weight,
    adapter_in,
    adapter_out,
    moment_in,
    square_in,
    moment_out,
    square_out,
):
    role = lax.axis_index("role")
    core = lax.axis_index("core")
    shard_index = lax.axis_index(HIDDEN)
    flags = jnp.stack([role, core, lax.axis_index("x")]).astype(jnp.int32)
    token_batch = token_rows[0]
    group_rows = token_batch.shape[0]
    slice_width = adapter_in.shape[1]
    cols = frozen_gate_up_weight.shape[2]
    token_part = lax.dynamic_slice_in_dim(token_batch, shard_index * slice_width, slice_width, 1)

    in_bf = adapter_in.astype(BF)
    out_bf = adapter_out.astype(BF)
    ranks = 2 * in_bf.shape[2]

    def to_rank(matrix):
        part = jnp.einsum("knq,rn->kqr", matrix, token_part, preferred_element_type=F32)
        return part.reshape(ranks, group_rows)

    reduced = plus_partner(to_rank(in_bf), "ylo", 1)
    row_weight = KEEP_RATE ** staleness.astype(F32)
    rows = rows_by_x(token_batch, cotangent, row_weight[:, None])
    rows = exchange(rows, "x")
    own_weight, own_down, reduced = lax.optimization_barrier((frozen_gate_up_weight, down_weight.T, reduced))

    other_half = swapped(own_weight, "role")
    other_down = swapped(own_down, "role")
    reduced = plus_partner(plus_partner(reduced, "zl", 1), "zl", 2)
    other_half, other_down, reduced = lax.optimization_barrier((other_half, other_down, reduced))
    weights = (own_weight, other_half, swapped(own_weight, "core"), swapped(other_half, "core"))
    down_pair = jnp.stack([own_down, other_down])
    downs = (down_pair, swapped(down_pair, "core"))
    reduced = plus_partner(reduced, "zh", 1)
    rows, reduced = lax.optimization_barrier((rows, reduced))
    pieces = exchange(partials(flags, rows, weights, downs), "x")
    reduced = plus_partner(reduced, "zh", 2).astype(BF)
    base, hidden_old, through_part, out_part = middle(flags, pieces, reduced, out_bf)

    down_first, _ = lax.optimization_barrier((down_pair, pieces))
    through = sum_first(spread(through_part, NEAR)).astype(BF)
    through = spread(through, "zh")
    through = sum_first(through).astype(BF)
    behind, ahead = shifted(down_first, "x", 1), shifted(down_first, "x", 3)
    across = shifted(behind, "x", 1)
    same_core = [behind, across, ahead]

    def to_both_halves(value):
        return value + lax.ppermute(value, "role", [(0, 1)])

    out_part = to_both_halves(out_part)
    in_part = ADAPTER_SCALE * jnp.dot(through, token_part, preferred_element_type=F32)
    in_part = to_both_halves(in_part.astype(BF))
    other_behind, other_ahead = swapped(behind, "core"), swapped(ahead, "core")
    packed = jnp.concatenate([out_part, in_part], axis=1)
    packed, same_core = lax.optimization_barrier((packed, same_core))
    grads = spread(packed, DP)
    other_across = swapped(same_core[1], "core")
    blocks = [down_pair, *same_core, downs[1], other_behind, other_across, other_ahead]
    old_parts = layer_call(old_kernel, group_rows, slice_width, blocks, flags, hidden_old)
    grads, old_parts = lax.optimization_barrier((grads, old_parts))
    grads = sum_first(grads)
    grad_in = grads[:, cols:].reshape(2, -1, slice_width).transpose(0, 2, 1)
    grad_out = grads[:, :cols].reshape(2, -1, cols)
    new_in, new_m_in, new_s_in = adam_update(adapter_in, grad_in, moment_in, square_in)
    new_out, new_m_out, new_s_out = adam_update(adapter_out, grad_out, moment_out, square_out)

    positions = jnp.arange(group_rows)
    live = jnp.logical_or(role == 0, positions < prefill_rows[0])

    def finish(total):
        total = total.astype(BF).T
        return jnp.where(live[:, None], total, jnp.zeros_like(total))

    old_parts = old_parts.reshape(4, 2, 4, slice_width, group_rows)
    side = lax.axis_index("ylo")
    give = swapped(lax.dynamic_index_in_dim(old_parts, 1 - side, 1, keepdims=False), "ylo")
    keep = lax.dynamic_index_in_dim(old_parts, side, 1, keepdims=False)
    pair = (keep.astype(F32) + give.astype(F32)).astype(BF)
    renewed = to_rank(new_in.astype(BF)).astype(BF)
    renewed = spread(renewed, NEAR)
    renewed = sum_first(spread(sum_first(renewed).astype(BF), "zh")).astype(BF)
    near_old = shifted_sum(pair, "zl")
    new_parts = layer_call(new_kernel, group_rows, slice_width, blocks, flags, base, renewed, new_out.astype(BF))
    near_new = sum_first(exchange(new_parts.reshape(8, 4, slice_width, group_rows), NEAR))
    near = jnp.stack([near_old, near_new], axis=1).astype(BF)
    layers = sum_first(exchange(near, "zh"))
    layer_old, layer_new = finish(layers[0]), finish(layers[1])
    return (
        layer_old[None],
        layer_new[None],
        new_in[None],
        new_out[None],
        new_m_in[None],
        new_s_in[None],
        new_m_out[None],
        new_s_out[None],
    )


def solution(mesh):
    fine = Mesh(mesh.devices.reshape(2, 4, 2, 4, 4, 2), ("role", "x", "core", "zh", "zl", "ylo"))
    wide = ("role", "x", "core")
    in_specs = (
        P("role", DP, None),
        P(DP, None),
        P(DP),
        P(DP),
        P(None, wide, HIDDEN),
        P(HIDDEN, wide),
        P(None, HIDDEN, None),
        P(None, None, HIDDEN),
        P(None, HIDDEN, None),
        P(None, HIDDEN, None),
        P(None, None, HIDDEN),
        P(None, None, HIDDEN),
    )
    out_specs = (
        P("role", DP, HIDDEN),
        P("role", DP, HIDDEN),
        P("role", None, HIDDEN, None),
        P("role", None, None, HIDDEN),
        P("role", None, HIDDEN, None),
        P("role", None, HIDDEN, None),
        P("role", None, None, HIDDEN),
        P("role", None, None, HIDDEN),
    )
    return jax.shard_map(step, mesh=fine, in_specs=in_specs, out_specs=out_specs, check_vma=False)
```

```python
import jax
import jax.numpy as jnp
from jax import lax
from jax.experimental import pallas as pl
from jax.experimental.pallas import tpu as pltpu
from jax.sharding import Mesh
from jax.sharding import PartitionSpec as P


D = 5120
OPT_STEP = 10

ADAPTER_SCALE = 2.0
BETA_ONE = 0.9
BETA_TWO = 0.999
RATE_FACTOR = 0.34
ADAM_EPS = 1e-08
KEEP_RATE = 0.75

DP = ("x", "core")
NEAR = ("zl", "ylo")
HIDDEN = ("zh", "zl", "ylo")
BF = jnp.bfloat16
F32 = jnp.float32


VMEM = pl.BlockSpec(memory_space=pltpu.VMEM)
SMEM = pl.BlockSpec(memory_space=pltpu.SMEM)
ANY = pl.BlockSpec(memory_space=pl.ANY)


def exchange(pieces, axis):
    return lax.all_to_all(pieces, axis, split_axis=0, concat_axis=0, tiled=True)


def swapped(value, axis):
    return lax.ppermute(value, axis, [(0, 1), (1, 0)])


def spread(value, axis):
    count = lax.axis_size(axis)
    return exchange(jnp.broadcast_to(value, (count, *value.shape)), axis)


def sum_first(pieces):
    return pieces.astype(F32).sum(axis=0)


def shifted(value, axis, step):
    count = lax.axis_size(axis)
    return lax.ppermute(value, axis, [(i, (i + step) % count) for i in range(count)])


def plus_partner(value, axis, step):
    count = lax.axis_size(axis)
    return value + lax.ppermute(value, axis, [(i, i ^ step) for i in range(count)])


def shifted_sum(pieces, axis):
    index = lax.axis_index(axis)
    count = lax.axis_size(axis)
    total = lax.dynamic_index_in_dim(pieces, index, 0, keepdims=False).astype(F32)
    for step in range(1, count):
        piece = lax.dynamic_index_in_dim(pieces, lax.rem(index + step, count), 0, keepdims=False)
        total = total + shifted(piece, axis, step).astype(F32)
    return total


def adam_update(param, grad, first, second):
    learn_rate = RATE_FACTOR / D**0.5
    first_new = BETA_ONE * first + (1.0 - BETA_ONE) * grad
    second_new = BETA_TWO * second + (1.0 - BETA_TWO) * grad * grad
    first_fix = first_new / (1.0 - BETA_ONE**OPT_STEP)
    second_fix = second_new / (1.0 - BETA_TWO**OPT_STEP)
    return (
        param - learn_rate * first_fix / (jnp.sqrt(second_fix) + ADAM_EPS),
        first_new,
        second_new,
    )


def dot(a, b, dims):
    return lax.dot_general(a, b, (dims, ((), ())), preferred_element_type=F32)


def rows_kernel(token_ref, cotangent_ref, scale_ref, out_ref):
    width = out_ref.shape[4]
    scale = scale_ref[...]
    for half in range(2):
        for x in range(4):
            columns = slice((half * 4 + x) * width, (half * 4 + x + 1) * width)
            out_ref[x, 0, half] = token_ref[:, columns]
            out_ref[x, 1, half] = (scale * cotangent_ref[:, columns].astype(F32)).astype(BF)


def rows_by_x(tokens, cotangent, scale):
    group, width = tokens.shape
    return pl.pallas_call(
        rows_kernel,
        out_shape=jax.ShapeDtypeStruct((4, 2, 2, group, width // 8), BF),
        in_specs=[VMEM, VMEM, VMEM],
        out_specs=VMEM,
        name="rows_by_x",
    )(tokens, cotangent, scale)


def partial_kernel(flag_ref, rows_ref, *refs):
    block_refs = refs[:4]
    out_ref, weight, held, in_sems, out_sems = refs[4:]
    role, core = flag_ref[0], flag_ref[1]
    depth = block_refs[0].shape[1]
    loads = []
    for i in range(2):
        side = core if i == 0 else 1 - core
        place = pl.ds(pl.multiple_of(side * depth, depth), depth)
        for j in range(2):
            half = role if j == 0 else 1 - role
            n = 2 * i + j
            loads.append(pltpu.make_async_copy(block_refs[n], weight.at[half, :, place, :], in_sems.at[n]))
    for copy in loads:
        copy.start()
    for copy in loads:
        copy.wait()

    count, group = rows_ref.shape[0], rows_ref.shape[3]

    def all_rows(which, half):
        return jnp.concatenate([rows_ref[x, which, half] for x in range(count)], axis=0)

    stores = []
    for k in range(3):
        total = 0.0
        for half in range(2):
            total += dot(all_rows(k // 2, half), weight[half, k], ((1,), (0,)))
        turned = total.astype(BF).T
        for x in range(count):
            held[k, x] = turned[:, x * group : (x + 1) * group]
        copy = pltpu.make_async_copy(held.at[k], out_ref.at[:, k], out_sems.at[k])
        copy.start()
        stores.append(copy)
    for copy in stores:
        copy.wait()


def partials(flags, rows, blocks):
    count, _, _, group, _ = rows.shape
    kinds, depth, cols = blocks[0].shape
    return pl.pallas_call(
        partial_kernel,
        out_shape=jax.ShapeDtypeStruct((count, kinds, cols, group), BF),
        in_specs=[SMEM, VMEM] + [ANY] * 4,
        out_specs=ANY,
        scratch_shapes=[
            pltpu.VMEM((2, kinds, 2 * depth, cols), BF),
            pltpu.VMEM((kinds, count, cols, group), BF),
            pltpu.SemaphoreType.DMA((4,)),
            pltpu.SemaphoreType.DMA((kinds,)),
        ],
        name="partials",
    )(flags, rows, *blocks)


def middle_kernel(flag_ref, pieces_ref, reduced_ref, lift_ref, base_ref, hidden_ref, through_ref, grad_ref):
    total = [pieces_ref[0, k].astype(F32) for k in range(3)]
    for x in range(1, pieces_ref.shape[0]):
        for k in range(3):
            total[k] = total[k] + pieces_ref[x, k].astype(F32)
    rank = lift_ref.shape[1]
    pre = []
    for k in range(2):
        base_ref[k] = total[k]
        part = reduced_ref[k * rank : (k + 1) * rank, :]
        pre.append(total[k] + ADAPTER_SCALE * dot(lift_ref[k], part, ((0,), (0,))))
    gate, up = pre
    sigma = jax.nn.sigmoid(gate)
    silu = gate * sigma
    hidden_ref[...] = (silu * up).astype(BF)
    grad_hidden = jnp.where(flag_ref[0] == 0, total[2], jnp.zeros_like(total[2]))
    grads = (
        (grad_hidden * up * sigma * (1.0 + gate * (1.0 - sigma))).astype(BF),
        (grad_hidden * silu).astype(BF),
    )
    for k in range(2):
        block = slice(k * rank, (k + 1) * rank)
        through_ref[block, :] = dot(lift_ref[k], grads[k], ((1,), (0,))).astype(BF)
        grad_ref[block, :] = (
            ADAPTER_SCALE * dot(reduced_ref[block, :], grads[k], ((1,), (1,)))
        ).astype(BF)


def middle(flags, pieces, reduced, lift):
    _, _, cols, group = pieces.shape
    ranks = reduced.shape[0]
    return pl.pallas_call(
        middle_kernel,
        out_shape=(
            jax.ShapeDtypeStruct((2, cols, group), F32),
            jax.ShapeDtypeStruct((cols, group), BF),
            jax.ShapeDtypeStruct((ranks, group), BF),
            jax.ShapeDtypeStruct((ranks, cols), BF),
        ),
        in_specs=[SMEM, VMEM, VMEM, VMEM],
        out_specs=(VMEM, VMEM, VMEM, VMEM),
        name="middle",
    )(flags, pieces, reduced, lift)


def down_product(flag_ref, hidden, block_refs, out_ref):
    role, x, core = flag_ref[0], flag_ref[2], flag_ref[1]
    size = out_ref.shape[1]
    for i in range(2):
        side = core if i == 0 else 1 - core
        for step in range(4):
            source = lax.rem(x + 4 - step, 4)
            for j in range(2):
                half = role if j == 0 else 1 - role
                product = dot(block_refs[4 * i + step][j], hidden, ((1,), (0,))).astype(BF)
                block = half * 8 + 2 * source + side
                for s in range(2):
                    place = 2 * block + s
                    out_ref[lax.rem(place, 8) * 4 + lax.div(place, 8)] = product[s * size : (s + 1) * size]


def old_kernel(flag_ref, hidden_ref, *refs):
    down_product(flag_ref, hidden_ref[...], refs[:-1], refs[-1])


def new_kernel(flag_ref, base_ref, reduced_ref, lift_ref, *refs):
    rank = lift_ref.shape[1]
    post = []
    for k in range(2):
        part = reduced_ref[k * rank : (k + 1) * rank, :]
        post.append(base_ref[k] + ADAPTER_SCALE * dot(lift_ref[k], part, ((0,), (0,))))
    hidden = (post[0] * jax.nn.sigmoid(post[0]) * post[1]).astype(BF)
    down_product(flag_ref, hidden, refs[:-1], refs[-1])


def layer_call(kernel, group, width, blocks, *operands):
    return pl.pallas_call(
        kernel,
        out_shape=jax.ShapeDtypeStruct((32, width, group), BF),
        in_specs=[SMEM] + [VMEM] * (len(operands) - 1 + len(blocks)),
        out_specs=VMEM,
    )(*operands, *blocks)


def step(
    token_rows,
    cotangent,
    staleness,
    prefill_rows,
    frozen_gate_up_weight,
    down_weight,
    adapter_in,
    adapter_out,
    moment_in,
    square_in,
    moment_out,
    square_out,
):
    role = lax.axis_index("role")
    core = lax.axis_index("core")
    shard_index = lax.axis_index(HIDDEN)
    flags = jnp.stack([role, core, lax.axis_index("x")]).astype(jnp.int32)
    token_batch = token_rows[0]
    group_rows = token_batch.shape[0]
    slice_width = adapter_in.shape[1]
    cols = frozen_gate_up_weight.shape[2]
    token_part = lax.dynamic_slice_in_dim(token_batch, shard_index * slice_width, slice_width, 1)

    in_bf = adapter_in.astype(BF)
    out_bf = adapter_out.astype(BF)
    ranks = 2 * in_bf.shape[2]

    def to_rank(matrix):
        part = jnp.einsum("knq,rn->kqr", matrix, token_part, preferred_element_type=F32)
        return part.reshape(ranks, group_rows)

    reduced = plus_partner(to_rank(in_bf), "ylo", 1)
    row_weight = KEEP_RATE ** staleness.astype(F32)
    rows = rows_by_x(token_batch, cotangent, row_weight[:, None])
    rows = exchange(rows, "x")
    own, reduced = lax.optimization_barrier(
        (jnp.concatenate([frozen_gate_up_weight, down_weight.T[None]]), reduced)
    )

    other = swapped(own, "role")
    reduced = plus_partner(plus_partner(reduced, "zl", 1), "zl", 2)
    other, reduced = lax.optimization_barrier((other, reduced))
    near_blocks = (own, other, swapped(own, "core"), swapped(other, "core"))
    reduced = plus_partner(reduced, "zh", 1)
    rows, reduced = lax.optimization_barrier((rows, reduced))
    pieces = exchange(partials(flags, rows, near_blocks), "x")
    reduced = plus_partner(reduced, "zh", 2).astype(BF)
    base, hidden_old, through_part, out_part = middle(flags, pieces, reduced, out_bf)

    later_blocks, _ = lax.optimization_barrier((near_blocks, pieces))
    down_first, down_core = (jnp.stack([a[2], b[2]]) for a, b in (later_blocks[:2], later_blocks[2:]))
    through = sum_first(spread(through_part, NEAR)).astype(BF)
    through = spread(through, "zh")
    through = sum_first(through).astype(BF)
    behind, ahead = shifted(down_first, "x", 1), shifted(down_first, "x", 3)
    across = shifted(behind, "x", 1)
    same_core = [behind, across, ahead]

    def to_both_halves(value):
        return value + lax.ppermute(value, "role", [(0, 1)])

    out_part = to_both_halves(out_part)
    in_part = ADAPTER_SCALE * jnp.dot(through, token_part, preferred_element_type=F32)
    in_part = to_both_halves(in_part.astype(BF))
    other_behind, other_ahead = swapped(behind, "core"), swapped(ahead, "core")
    packed = jnp.concatenate([out_part, in_part], axis=1)
    packed, same_core = lax.optimization_barrier((packed, same_core))
    grads = spread(packed, DP)
    other_across = swapped(same_core[1], "core")
    blocks = [down_first, *same_core, down_core, other_behind, other_across, other_ahead]
    old_parts = layer_call(old_kernel, group_rows, slice_width, blocks, flags, hidden_old)
    grads, old_parts = lax.optimization_barrier((grads, old_parts))
    grads = sum_first(grads)
    grad_in = grads[:, cols:].reshape(2, -1, slice_width).transpose(0, 2, 1)
    grad_out = grads[:, :cols].reshape(2, -1, cols)
    new_in, new_m_in, new_s_in = adam_update(adapter_in, grad_in, moment_in, square_in)
    new_out, new_m_out, new_s_out = adam_update(adapter_out, grad_out, moment_out, square_out)

    positions = jnp.arange(group_rows)
    live = jnp.logical_or(role == 0, positions < prefill_rows[0])

    def finish(total):
        total = total.astype(BF).T
        return jnp.where(live[:, None], total, jnp.zeros_like(total))

    old_parts = old_parts.reshape(4, 2, 4, slice_width, group_rows)
    side = lax.axis_index("ylo")
    give = swapped(lax.dynamic_index_in_dim(old_parts, 1 - side, 1, keepdims=False), "ylo")
    keep = lax.dynamic_index_in_dim(old_parts, side, 1, keepdims=False)
    pair = (keep.astype(F32) + give.astype(F32)).astype(BF)
    renewed = to_rank(new_in.astype(BF)).astype(BF)
    renewed = spread(renewed, NEAR)
    renewed = sum_first(spread(sum_first(renewed).astype(BF), "zh")).astype(BF)
    near_old = shifted_sum(pair, "zl")
    new_parts = layer_call(
        new_kernel, group_rows, slice_width, blocks, flags, base, renewed, new_out.astype(BF)
    )
    near_new = sum_first(exchange(new_parts.reshape(8, 4, slice_width, group_rows), NEAR))
    near = jnp.stack([near_old, near_new], axis=1).astype(BF)
    layers = sum_first(exchange(near, "zh"))
    layer_old, layer_new = finish(layers[0]), finish(layers[1])
    return (
        layer_old[None],
        layer_new[None],
        new_in[None],
        new_out[None],
        new_m_in[None],
        new_s_in[None],
        new_m_out[None],
        new_s_out[None],
    )


def solution(mesh):
    fine = Mesh(mesh.devices.reshape(2, 4, 2, 4, 4, 2), ("role", "x", "core", "zh", "zl", "ylo"))
    wide = ("role", "x", "core")
    in_specs = (
        P("role", DP, None),
        P(DP, None),
        P(DP),
        P(DP),
        P(None, wide, HIDDEN),
        P(HIDDEN, wide),
        P(None, HIDDEN, None),
        P(None, None, HIDDEN),
        P(None, HIDDEN, None),
        P(None, HIDDEN, None),
        P(None, None, HIDDEN),
        P(None, None, HIDDEN),
    )
    out_specs = (
        P("role", DP, HIDDEN),
        P("role", DP, HIDDEN),
        P("role", None, HIDDEN, None),
        P("role", None, None, HIDDEN),
        P("role", None, HIDDEN, None),
        P("role", None, HIDDEN, None),
        P("role", None, None, HIDDEN),
        P("role", None, None, HIDDEN),
    )
    return jax.shard_map(step, mesh=fine, in_specs=in_specs, out_specs=out_specs, check_vma=False)
```
